32 devices in a mesh: energy: 8 (over z, x), slab: 4 (over y, core).
Axes of the slice: x: 2, y: 2, z: 4, core: 2. Of those that a mesh axis runs over, the one named last changes fastest.
Arguments:
- hamilton: float32 [4, 2, 256, 256], P('slab'), as said below
- couple: float32 [4, 2, 256, 256], P('slab'), may hold values from -0.125 to 0.125
- lead_left: float32 [2, 256, 256], replicated, may hold values from -0.25 to 0.25
- rates: float32 [8, 4, 256], P('energy', 'slab'), may hold values from 0.1 to 1
- fill: float32 [2, 8], P(None, 'energy'), may hold values from 0.05 to 0.95
- sigma_less: float32 [8, 4, 2, 256, 256], P('energy', 'slab'), as said below
- strength: float32 [2, 256, 256], replicated, may hold values from 0.1 to 1
- phonon_fill: float32 [2], replicated, may hold values from 0.2 to 2
- phonon_shift: int32 [2], replicated, may hold values from 1 to 6
Outputs:
- lesser_green: float32 [8, 4, 2, 256, 256], P('energy', 'slab')
- scatter_less: float32 [8, 4, 2, 256, 256], P('energy', 'slab')
The draws below stay inside these ranges and needn't reach their ends.
Inputs may be any that keep to these rules, and one draw needn't show every extreme that they name: Each block of hamilton is Hermitian. Each block of sigma_less is anti-Hermitian.
All inputs are finite; a program needn't handle non-finite values.
Results may differ from the reference program's by a relative error of at most 0.00025.
Values sent between devices are 32-bit elements; how exact they have to be, the bound alone decides.
No kernel may reach another device: no remote copies, remote signals or barrier semaphores. Data moves between devices by JAX's collectives and lax.ppermute only.
A program may use at most 128 MiB of HBM per device.

```python
import math
import jax
import jax.numpy as jnp
from jax import lax

ORB = 256
E_DEV = 1
NMODE = 2
ENERGIES = 8
SLICES = 4


def draw_hamilton(key, part):
    first_key, second_key = jax.random.split(jax.random.fold_in(key, 11))
    draw_shape = (SLICES, ORB, ORB)
    first_raw = jax.random.normal(first_key, draw_shape, jnp.float32)
    second_raw = jax.random.normal(second_key, draw_shape, jnp.float32)
    factor = 0.5 / math.sqrt(ORB)
    real_part = (first_raw + jnp.swapaxes(first_raw, 1, 2)) * factor
    imag_part = (second_raw - jnp.swapaxes(second_raw, 1, 2)) * factor
    return jnp.stack([real_part, imag_part], axis=1)


def draw_sigma_less(key, part):
    first_key, second_key = jax.random.split(jax.random.fold_in(key, 23))
    draw_shape = (ENERGIES, SLICES, ORB, ORB)
    first_raw = jax.random.normal(first_key, draw_shape, jnp.float32)
    second_raw = jax.random.normal(second_key, draw_shape, jnp.float32)
    factor = 0.2 / math.sqrt(ORB)
    symmetric = (first_raw + jnp.swapaxes(first_raw, 2, 3)) * factor
    skewed = (second_raw - jnp.swapaxes(second_raw, 2, 3)) * factor
    return jnp.stack([-skewed, symmetric], axis=2)


def draw_phonon_shift(key, part):
    first_key, second_key = jax.random.split(jax.random.fold_in(key, 37))
    largest = 7 * E_DEV - 1
    other = jax.random.randint(first_key, (), 1, largest + 1)
    flipped = jax.random.randint(second_key, (), 0, 2)
    top = jnp.full((), largest, jnp.int32)
    return jnp.where(flipped == 1, jnp.stack([top, other]), jnp.stack([other, top])).astype(jnp.int32)


def levels(key, shape, pieces, smallest, top_value):
    def one(axis_at, blocks):
        draws = jax.random.uniform(jax.random.fold_in(jax.random.fold_in(key, 6), axis_at), (blocks,), jnp.float32, smallest / len(pieces), top_value / len(pieces))
        return jnp.repeat(jnp.exp(draws), shape[axis_at] // blocks).reshape((-1,) + (1,) * (len(shape) - axis_at - 1))

    level = one(*pieces[0])
    for cut in pieces[1:]:
        level = level * one(*cut)
    return level


def gaussian(own_key, dims, width, most, cuts=(), held_as=jnp.bfloat16):
    loudness = levels(own_key, dims, cuts, -0.22, 0.18) if cuts else 1.0
    entries = jax.random.normal(own_key, dims, jnp.float32) * width * loudness
    return jnp.minimum(jnp.maximum(entries, -most), most).astype(held_as)


def setup_inputs(seed: int = 0) -> dict:
    splits = jax.random.split(jax.random.key(seed), 10)
    return {
        "hamilton": draw_hamilton(jax.random.fold_in(splits[9], 71), 0),
        "couple": gaussian(splits[1], (SLICES, 2, ORB, ORB), (8 * ORB) ** -0.5, 0.125, ((0, 4),), jnp.float32),
        "lead_left": gaussian(splits[2], (2, ORB, ORB), (2 * ORB) ** -0.5, 0.25, (), jnp.float32),
        "rates": jnp.clip(jnp.exp(math.log(1.0) - 2.3025851 * jax.random.uniform(splits[3], (ENERGIES, SLICES, ORB), jnp.float32) ** levels(splits[3], (ENERGIES, SLICES, ORB), ((0, 8), (1, 4)), -0.2, 0.2)), 0.1, 1.0),
        "fill": jnp.clip(0.05 + 0.9 * jax.random.uniform(splits[4], (2, ENERGIES), jnp.float32) ** levels(splits[4], (2, ENERGIES), ((1, 8),), -0.2, 0.2), 0.05, 0.95),
        "sigma_less": draw_sigma_less(jax.random.fold_in(splits[9], 71), 0),
        "strength": jnp.clip(jnp.exp(jax.random.uniform(splits[6], (NMODE, ORB, ORB), jnp.float32, math.log(0.1), math.log(1.0))), 0.1, 1.0),
        "phonon_fill": jnp.clip(jnp.exp(jax.random.uniform(splits[7], (NMODE,), jnp.float32, math.log(0.2), math.log(2.0))), 0.2, 2.0),
        "phonon_shift": draw_phonon_shift(jax.random.fold_in(splits[9], 71), 0),
    }


ETA = 0.2
EMIN = -2.5
ESPAN = 5.0

def matmul_hi(left_op, right_op):
    return jnp.matmul(left_op, right_op, precision=lax.Precision.HIGHEST)

def matmul_nt(left_op, right_op):
    return jnp.einsum('...ij,...kj->...ik', left_op, right_op, precision=lax.Precision.HIGHEST)

def matmul_tn(left_op, right_op):
    return jnp.einsum('...ji,...jk->...ik', left_op, right_op, precision=lax.Precision.HIGHEST)

def complex_mul(first_op, second_op):
    real_first = first_op[..., 0, :, :]
    imag_first = first_op[..., 1, :, :]
    real_second = second_op[..., 0, :, :]
    imag_second = second_op[..., 1, :, :]
    real_part = matmul_hi(real_first, real_second) - matmul_hi(imag_first, imag_second)
    imag_part = matmul_hi(real_first, imag_second) + matmul_hi(imag_first, real_second)
    return jnp.stack([real_part, imag_part], axis=-3)

def complex_mul_nt(first_op, second_op):
    real_first = first_op[..., 0, :, :]
    imag_first = first_op[..., 1, :, :]
    real_second = second_op[..., 0, :, :]
    imag_second = second_op[..., 1, :, :]
    real_part = matmul_nt(real_first, real_second) + matmul_nt(imag_first, imag_second)
    imag_part = matmul_nt(imag_first, real_second) - matmul_nt(real_first, imag_second)
    return jnp.stack([real_part, imag_part], axis=-3)

def complex_mul_tn(first_op, second_op):
    real_first = first_op[..., 0, :, :]
    imag_first = first_op[..., 1, :, :]
    real_second = second_op[..., 0, :, :]
    imag_second = second_op[..., 1, :, :]
    real_part = matmul_tn(real_first, real_second) + matmul_tn(imag_first, imag_second)
    imag_part = matmul_tn(real_first, imag_second) - matmul_tn(imag_first, real_second)
    return jnp.stack([real_part, imag_part], axis=-3)

def dagger(matrix):
    return jnp.stack([jnp.swapaxes(matrix[..., 0, :, :], -1, -2), -jnp.swapaxes(matrix[..., 1, :, :], -1, -2)], axis=-3)

def complex_inverse(matrix):
    real_part = matrix[..., 0, :, :]
    imag_part = matrix[..., 1, :, :]
    orbitals = real_part.shape[-1]
    upper = jnp.concatenate([real_part, -imag_part], axis=-1)
    lower = jnp.concatenate([imag_part, real_part], axis=-1)
    embedded = jnp.concatenate([upper, lower], axis=-2)
    normal = matmul_tn(embedded, embedded)
    factor = jnp.linalg.cholesky(normal)
    solved = jax.scipy.linalg.cho_solve((factor, True), jnp.swapaxes(upper, -1, -2))
    return jnp.stack([solved[..., :orbitals, :], solved[..., orbitals:, :]], axis=-3)

def times_imag(matrix, factor):
    return jnp.stack([-factor * matrix[1], factor * matrix[0]], axis=-3)

def left_matrix(energies, rate_rows, hamilton_slice, boundary_ret):
    orbitals = hamilton_slice.shape[-1]
    identity = jnp.eye(orbitals, dtype=jnp.float32)
    real_part = energies[:, None, None] * identity - hamilton_slice[0] - boundary_ret[:, 0]
    imag_part = (ETA + rate_rows)[:, None, :] * identity - hamilton_slice[1] - boundary_ret[:, 1]
    return jnp.stack([real_part, imag_part], axis=1)

def backward_step(green, lesser, couple_slice, next_ret, next_less):
    across = complex_mul(green, couple_slice)
    right_ret = complex_mul_tn(couple_slice, green)
    right_less = complex_mul_tn(couple_slice, lesser)
    full = green + complex_mul(across, complex_mul(next_ret, right_ret))
    mixed = complex_mul(across, complex_mul(next_ret, right_less))
    full_less = lesser + complex_mul_nt(complex_mul(across, next_less), across) + mixed - dagger(mixed)
    return (full, full_less)

def reference(hamilton, couple, lead_left, rates, fill, sigma_less, strength, phonon_fill, phonon_shift):
    orbitals = hamilton.shape[-1]
    energies = jnp.arange(ENERGIES, dtype=jnp.int32).astype(jnp.float32) * (ESPAN / ENERGIES) + EMIN
    gamma_left = complex_mul_nt(lead_left, lead_left)
    gamma_right = complex_mul_nt(couple[SLICES - 1], couple[SLICES - 1])
    edge_ret = jnp.zeros((ENERGIES, 2, orbitals, orbitals), jnp.float32)
    edge_less = jnp.zeros((ENERGIES, 2, orbitals, orbitals), jnp.float32)
    greens = []
    lessers = []
    for slice_index in range(SLICES):
        matrix = left_matrix(energies, rates[:, slice_index], hamilton[slice_index], edge_ret)
        source = sigma_less[:, slice_index] + edge_less
        if slice_index == 0:
            matrix = matrix + times_imag(gamma_left, 0.5)
            source = source + times_imag(gamma_left, fill[0][:, None, None])
        if slice_index == SLICES - 1:
            matrix = matrix + times_imag(gamma_right, 0.5)
            source = source + times_imag(gamma_right, fill[1][:, None, None])
        green = complex_inverse(matrix)
        lesser = complex_mul_nt(complex_mul(green, source), green)
        greens.append(green)
        lessers.append(lesser)
        edge_ret = complex_mul(complex_mul_tn(couple[slice_index], green), couple[slice_index])
        edge_less = complex_mul(complex_mul_tn(couple[slice_index], lesser), couple[slice_index])
    next_ret = jnp.zeros((ENERGIES, 2, orbitals, orbitals), jnp.float32)
    next_less = jnp.zeros((ENERGIES, 2, orbitals, orbitals), jnp.float32)
    results = [None] * SLICES
    for slice_index in reversed(range(SLICES)):
        next_ret, next_less = backward_step(greens[slice_index], lessers[slice_index], couple[slice_index], next_ret, next_less)
        results[slice_index] = next_less
    lesser_green = jnp.stack(results, axis=1)
    padding = jnp.zeros_like(lesser_green)
    padded_up = jnp.concatenate([lesser_green, padding], axis=0)
    padded_down = jnp.concatenate([padding, lesser_green], axis=0)
    summed = jnp.zeros_like(lesser_green)
    for mode_index in range(NMODE):
        shifted_up = lax.dynamic_slice_in_dim(padded_up, phonon_shift[mode_index].astype(jnp.int32), ENERGIES, 0)
        shifted_down = lax.dynamic_slice_in_dim(padded_down, (ENERGIES - phonon_shift[mode_index]).astype(jnp.int32), ENERGIES, 0)
        summed = summed + strength[mode_index] * ((phonon_fill[mode_index] + 1.0) * shifted_up + phonon_fill[mode_index] * shifted_down)
    return (lesser_green, summed)
```

```python
import jax
import jax.numpy as jnp
from jax import lax
from jax.experimental import pallas as pl
from jax.experimental.pallas import tpu as pltpu
from jax.sharding import PartitionSpec as P

ETA = 0.2
EMIN = -2.5
ESPAN = 5.0
LARGEST_SHIFT = 6
POLY_STEPS = 5
POLY_RANGE = 110.0
ACCEPT = 1e-3
SLOW_STEPS = 80

F32 = jnp.float32
BF16 = jnp.bfloat16


def dot(a, b):
    return jnp.dot(a, b, preferred_element_type=F32)


def dot_nt(a, b):
    return lax.dot_general(a, b, (((1,), (1,)), ((), ())), preferred_element_type=F32)


def dot_tn(a, b):
    return lax.dot_general(a, b, (((0,), (0,)), ((), ())), preferred_element_type=F32)


def cols(*parts):
    return jnp.concatenate(parts, axis=1)


def rows(*parts):
    return jnp.concatenate(parts, axis=0)


def split(pair):
    high = tuple(part.astype(BF16) for part in pair)
    low = tuple((part - top.astype(F32)).astype(BF16) for part, top in zip(pair, high))
    return high, low


def rounded(pair):
    return tuple(part.astype(BF16) for part in pair)


def left_form(pair):
    return cols(pair[0], pair[1])


def right_form(pair):
    return rows(cols(pair[0], pair[1]), cols(-pair[1], pair[0]))


def halves_cols(wide):
    size = wide.shape[1] // 2
    return wide[:, :size], wide[:, size:]


def halves_rows(tall):
    size = tall.shape[0] // 2
    return tall[:size], tall[size:]


def product_one(a, b):
    return halves_cols(dot(left_form(a), right_form(b)))


def product_split(a_high, a_low, b_high, b_low):
    top, right = left_form(a_high), right_form(b_high)
    return halves_cols(
        dot(cols(top, top, left_form(a_low)), rows(right, right_form(b_low), right))
    )


def product(a, b):
    return product_split(*split(a), *split(b))


def product_nt(a, b):
    def stacked(pair):
        return rows(cols(pair[0], pair[1]), cols(pair[1], -pair[0]))

    a_high, a_low = split(a)
    b_high, b_low = split(b)
    top, right = stacked(a_high), left_form(b_high)
    return halves_rows(
        dot_nt(cols(top, top, stacked(a_low)), cols(right, left_form(b_low), right))
    )


def product_tn(a, b):
    def tall(pair):
        return rows(pair[0], pair[1])

    def stacked(pair):
        return rows(cols(pair[0], pair[1]), cols(pair[1], -pair[0]))

    a_high, a_low = split(a)
    b_high, b_low = split(b)
    top, right = tall(a_high), stacked(b_high)
    return halves_cols(
        dot_tn(rows(top, top, tall(a_low)), rows(right, stacked(b_low), right))
    )


def minus(a, b):
    return (a[0] - b[0], a[1] - b[1])


def plus(a, b):
    return (a[0] + b[0], a[1] + b[1])


def dagger(a):
    return (a[0].T, -a[1].T)


def load(ref):
    return (ref[0], ref[1])


def save(ref, pair):
    ref[0] = pair[0]
    ref[1] = pair[1]


def square_sum(pair):
    return jnp.sum(pair[0] * pair[0] + pair[1] * pair[1])


def row_col(size):
    shape = (size, size)
    return lax.broadcasted_iota(jnp.int32, shape, 0), lax.broadcasted_iota(jnp.int32, shape, 1)


def identity(size):
    row, col = row_col(size)
    return (row == col).astype(F32)


def pack(pair):
    row, col = row_col(pair[0].shape[0])
    return jnp.where(row > col, pair[0], pair[1])


def unpack(packed):
    row, col = row_col(packed.shape[0])
    flipped = packed.T
    real = jnp.where(row > col, packed, jnp.where(row < col, -flipped, 0.0))
    imag = jnp.where(row > col, flipped, packed)
    return (real, imag)


def scalings():
    low, high, found = 1.0 / POLY_RANGE, 1.0, []
    for _ in range(POLY_STEPS):
        rate = (high - low) / (high + low)
        found.append(2.0 / (low + high))
        low, high = 1.0 - rate * rate, 1.0
    return found


def invert(matrix, out_ref):
    size = matrix[0].shape[0]
    high, low = split(matrix)
    adjoint = dagger(matrix)
    adjoint_16 = rounded(adjoint)
    state = product_one(adjoint_16, high)
    state_16 = rounded(state)
    both = dot(left_form(state_16), cols(right_form(state_16), right_form(adjoint_16)))
    squared = halves_cols(both[:, : 2 * size])
    moved = halves_cols(both[:, 2 * size :])
    inverse_bound = lax.rsqrt(jnp.sqrt(square_sum(squared)))
    scales = scalings()
    once, twice = 2.0 * scales[0] * inverse_bound, scales[0] ** 2 * inverse_bound**2
    guess = tuple(once * a - twice * q for a, q in zip(adjoint, moved))
    state = tuple(once * s - twice * q for s, q in zip(state, squared))
    for step in range(1, POLY_STEPS):
        once, twice = 2.0 * scales[step], scales[step] ** 2
        state_16, guess_16 = rounded(state), rounded(guess)
        if step < POLY_STEPS - 1:
            both = dot(left_form(state_16), cols(right_form(state_16), right_form(guess_16)))
            squared = halves_cols(both[:, : 2 * size])
            moved = halves_cols(both[:, 2 * size :])
            state = tuple(once * s - twice * q for s, q in zip(state, squared))
        else:
            moved = product_one(state_16, guess_16)
        guess = tuple(once * g - twice * q for g, q in zip(guess, moved))
    guess_high, guess_low = split(guess)
    made = product_split(high, low, guess_high, guess_low)
    residual = (identity(size) - made[0], -made[1])
    residual_16 = rounded(residual)
    second = product_one(residual_16, residual_16)
    fix = product_one(guess_high, rounded(plus(residual, second)))
    save(out_ref, plus(guess, fix))
    good = square_sum(second) < ACCEPT

    @pl.when(jnp.logical_not(good))
    def _():
        square = product(adjoint, matrix)
        bound = jnp.sqrt(square_sum(square))
        save(out_ref, (adjoint[0] / bound, adjoint[1] / bound))

        def more(carry):
            step, left_over = carry
            return jnp.logical_and(step < SLOW_STEPS, jnp.logical_not(left_over < 1e-6))

        def refine(carry):
            step, _ = carry
            now = load(out_ref)
            made = product(matrix, now)
            residual = (identity(size) - made[0], -made[1])
            save(out_ref, plus(now, product(now, residual)))
            return step + 1, square_sum(residual)

        lax.while_loop(more, refine, (jnp.int32(0), jnp.float32(1e30)))


def is_outer():
    place = lax.axis_index("slab")
    return jnp.logical_or(place == 0, place == lax.axis_size("slab") - 1)


def on_left():
    return lax.axis_index("slab") < lax.axis_size("slab") // 2


def first_kernel(step_width, hamilton, couple, lead_left, rates, matrix_ref, gamma_ref, green_ref, send_ref):
    size = hamilton.shape[-1]
    energy = lax.axis_index("energy").astype(F32) * step_width + EMIN
    eye = identity(size)
    real = energy * eye - hamilton[0, 0]
    imag = (ETA + rates[0]) * eye - hamilton[0, 1]

    @pl.when(jnp.logical_not(is_outer()))
    def _():
        save(matrix_ref, (real, imag))

    @pl.when(is_outer())
    def _():
        first = lax.axis_index("slab") == 0
        lead = tuple(jnp.where(first, lead_left[part], couple[0, part]) for part in range(2))
        gamma = product_nt(lead, lead)
        save(gamma_ref, gamma)
        matrix = (real - 0.5 * gamma[1], imag + 0.5 * gamma[0])
        invert(matrix, green_ref)

        @pl.when(first)
        def _():
            own = load(couple.at[0])
            save(send_ref, product(product_tn(own, load(green_ref)), own))

        @pl.when(jnp.logical_not(first))
        def _():
            save(send_ref, load(green_ref))


def first_less_kernel(sigma, gamma_ref, fill, couple, green_ref, less_ref, send_ref):
    @pl.when(is_outer())
    def _():
        first = lax.axis_index("slab") == 0
        occupation = jnp.where(first, fill[0, 0], fill[1, 0])
        source = (
            sigma[0, 0, 0] - occupation * gamma_ref[1],
            sigma[0, 0, 1] + occupation * gamma_ref[0],
        )
        green = load(green_ref)
        less = product_nt(product(green, source), green)
        save(less_ref, less)

        @pl.when(first)
        def _():
            own = load(couple.at[0])
            send_ref[...] = pack(product(product_tn(own, less), own))

        @pl.when(jnp.logical_not(first))
        def _():
            send_ref[...] = pack(less)


def second_kernel(matrix_in, edge, couple, matrix_ref, green_ref, send_ref):
    @pl.when(jnp.logical_not(is_outer()))
    def _():
        @pl.when(on_left())
        def _():
            save(matrix_ref, minus(load(matrix_in), load(edge)))

        @pl.when(jnp.logical_not(on_left()))
        def _():
            own = load(couple.at[0])
            around = product_nt(product(own, load(edge)), own)
            save(matrix_ref, minus(load(matrix_in), around))

        invert(load(matrix_ref), green_ref)

        @pl.when(on_left())
        def _():
            own = load(couple.at[0])
            save(send_ref, product(product_tn(own, load(green_ref)), own))

        @pl.when(jnp.logical_not(on_left()))
        def _():
            save(send_ref, load(green_ref))


def second_less_kernel(sigma, edge, couple, couple_before, green_ref, source_ref, send_ref):
    @pl.when(jnp.logical_not(is_outer()))
    def _():
        came = unpack(edge[...])
        own_sigma = (sigma[0, 0, 0], sigma[0, 0, 1])

        @pl.when(on_left())
        def _():
            save(source_ref, plus(own_sigma, came))

        @pl.when(jnp.logical_not(on_left()))
        def _():
            own = load(couple.at[0])
            save(source_ref, plus(own_sigma, product_nt(product(own, came), own)))

        green = load(green_ref)
        less = product_nt(product(green, load(source_ref)), green)

        @pl.when(on_left())
        def _():
            own = load(couple.at[0])
            send_ref[...] = pack(product(product_tn(own, less), own))

        @pl.when(jnp.logical_not(on_left()))
        def _():
            before = load(couple_before)
            send_ref[...] = pack(product_nt(product(before, less), before))


def third_kernel(matrix_in, edge, couple, matrix_ref, green_ref):
    @pl.when(jnp.logical_not(is_outer()))
    def _():
        @pl.when(on_left())
        def _():
            own = load(couple.at[0])
            around = product_nt(product(own, load(edge)), own)
            save(matrix_ref, minus(load(matrix_in), around))

        @pl.when(jnp.logical_not(on_left()))
        def _():
            save(matrix_ref, minus(load(matrix_in), load(edge)))

        invert(load(matrix_ref), green_ref)


def third_less_kernel(source, edge, green_ref, less_ref, send_ref):
    @pl.when(jnp.logical_not(is_outer()))
    def _():
        total = plus(load(source), unpack(edge[...]))
        green = load(green_ref)
        less = product_nt(product(green, total), green)
        save(less_ref, less)
        send_ref[...] = pack(less)


def prepare_kernel(couple, couple_before, green_ref, less_ref, across_ref, right_ref):
    @pl.when(is_outer())
    def _():
        @pl.when(on_left())
        def _():
            own = load(couple.at[0])
            save(across_ref, product(load(green_ref), own))
            save(right_ref, product_tn(own, load(less_ref)))

        @pl.when(jnp.logical_not(on_left()))
        def _():
            before = load(couple_before)
            save(across_ref, product_nt(load(green_ref), before))
            save(right_ref, product(before, load(less_ref)))


def mixed_kernel(across_ref, right_ref, less_ref, inner_green, base_ref):
    @pl.when(is_outer())
    def _():
        mixed = product(product(load(across_ref), load(inner_green)), load(right_ref))
        save(base_ref, minus(plus(load(less_ref), mixed), dagger(mixed)))


def last_kernel(across_ref, base_ref, inner_less, own_less, own_packed, out_ref, packed_ref):
    @pl.when(is_outer())
    def _():
        across = load(across_ref)
        less = plus(
            load(base_ref), product_nt(product(across, unpack(inner_less[...])), across)
        )
        save(out_ref, less)
        packed_ref[...] = pack(less)

    @pl.when(jnp.logical_not(is_outer()))
    def _():
        save(out_ref, load(own_less))
        packed_ref[...] = own_packed[...]


def scatter_kernel(low_up, low_down, high_up, high_down, strength, phonon_fill, phonon_shift, out_ref):
    swapped = (phonon_shift[0] > phonon_shift[1]).astype(jnp.int32)
    total = None
    for up, down, mode in ((low_up, low_down, swapped), (high_up, high_down, 1 - swapped)):
        filled = phonon_fill[mode]
        real, imag = unpack((filled + 1.0) * up[...] + filled * down[...])
        weight = strength[mode]
        term = (weight * real, weight * imag)
        total = term if total is None else plus(total, term)
    save(out_ref, total)


def call(body, name, outs, flops, smem, *args):
    where = [
        pl.BlockSpec(memory_space=pltpu.SMEM if index in smem else pltpu.VMEM)
        for index in range(len(args))
    ]
    return pl.pallas_call(
        body,
        out_shape=outs,
        in_specs=where,
        out_specs=[pl.BlockSpec(memory_space=pltpu.VMEM)] * len(outs),
        compiler_params=pltpu.CompilerParams(vmem_limit_bytes=40 << 20),
        cost_estimate=pl.CostEstimate(flops=flops, bytes_accessed=4 << 20, transcendentals=0),
        name=name,
    )(*args)


def hop(block, axis, pairs):
    return lax.ppermute(block, axis, pairs)


def shifted(block, distance):
    count = lax.axis_size("energy")
    up = [(i + distance, i) for i in range(count) if i + distance < count]
    down = [(i, i + distance) for i in range(count) if i + distance < count]
    return hop(block, "energy", up), hop(block, "energy", down)


def exchange(packed, phonon_shift):
    low = jnp.minimum(phonon_shift[0], phonon_shift[1]) - 1
    high = jnp.maximum(phonon_shift[0], phonon_shift[1]) - 1
    count = LARGEST_SHIFT
    which = low * count - low * (low - 1) // 2 + high - low
    branches = []
    for first in range(1, count + 1):
        for second in range(first, count + 1):

            def branch(block, first=first, second=second):
                near = shifted(block, first)
                far = near if second == first else shifted(block, second)
                return (*near, *far)

            branches.append(branch)
    return lax.switch(which, branches, packed)


def on_device(
    hamilton, couple, lead_left, rates, fill, sigma_less, strength, phonon_fill, phonon_shift
):
    e_dev, s_dev, _, size, _ = sigma_less.shape
    n_slab = lax.axis_size("slab")
    assert e_dev == 1 and s_dev == 1 and n_slab == 4
    step_width = ESPAN / (e_dev * lax.axis_size("energy"))
    full = jax.ShapeDtypeStruct((2, size, size), F32)
    half = jax.ShapeDtypeStruct((size, size), F32)
    inward = [(0, 1), (3, 2)]
    across_middle = [(1, 2), (2, 1)]
    outward = [(1, 0), (2, 3)]
    unit = 24 * size**3

    couple_before = hop(couple[0], "slab", [(1, 2), (2, 3)])

    def first_body(*refs):
        first_kernel(step_width, *refs)

    matrix, gamma, green, sent = call(
        first_body, "first", [full] * 4, 9 * unit, (), hamilton, couple, lead_left, rates[0]
    )
    edge = hop(sent, "slab", inward)
    less, sent = call(
        first_less_kernel, "first_less", [full, half], 4 * unit, (2,), sigma_less, gamma, fill, couple, green
    )
    edge_less = hop(sent, "slab", inward)
    edge, sent = lax.optimization_barrier((edge, sent))
    matrix, inner_green, sent = call(
        second_kernel, "second", [full] * 3, 10 * unit, (), matrix, edge, couple
    )
    edge = hop(sent, "slab", across_middle)
    source, sent = call(
        second_less_kernel, "second_less", [full, half], 6 * unit, (), sigma_less, edge_less, couple, couple_before, inner_green
    )
    edge_less = hop(sent, "slab", across_middle)
    across, right = call(
        prepare_kernel, "prepare", [full] * 2, 2 * unit, (), couple, couple_before, green, less
    )
    edge, sent, across, right = lax.optimization_barrier((edge, sent, across, right))
    _, inner_green = call(third_kernel, "third", [full] * 2, 8 * unit, (), matrix, edge, couple)
    came_green = hop(inner_green, "slab", outward)
    own_less, own_packed = call(
        third_less_kernel, "third_less", [full, half], 2 * unit, (), source, edge_less, inner_green
    )
    came_less = hop(own_packed, "slab", outward)
    (base,) = call(
        mixed_kernel, "mixed", [full], 2 * unit, (), across, right, less, came_green
    )
    lesser, packed = call(
        last_kernel, "last", [full, half], 2 * unit, (), across, base, came_less, own_less, own_packed
    )
    around = exchange(packed, phonon_shift)
    (scatter,) = call(
        scatter_kernel, "scatter", [full], unit // 8, (5, 6), *around, strength, phonon_fill, phonon_shift
    )
    return (lesser[None, None], scatter[None, None])


def solution(mesh):
    return jax.shard_map(
        on_device,
        mesh=mesh,
        in_specs=(
            P("slab", None, None, None),
            P("slab", None, None, None),
            P(),
            P("energy", "slab", None),
            P(None, "energy"),
            P("energy", "slab", None, None, None),
            P(),
            P(),
            P(),
        ),
        out_specs=(P("energy", "slab", None, None, None), P("energy", "slab", None, None, None)),
        check_vma=False,
    )
```

```python
import jax
import jax.numpy as jnp
import numpy as np
from jax import lax
from jax.experimental import pallas as pl
from jax.experimental.pallas import tpu as pltpu
from jax.sharding import PartitionSpec as P

ETA = 0.2
EMIN = -2.5
ESPAN = 5.0
LARGEST_SHIFT = 6
POLY_STEPS = 5
POLY_RANGE = 90.0
NORM_SHARE = 4.0
ACCEPT = 1e-3
SLOW_STEPS = 80
ROUNDS = 4
FETCH = "fetch"
FAR = pltpu.MemorySpace.HBM

F32 = jnp.float32
BF16 = jnp.bfloat16


def dot(a, b):
    return jnp.dot(a, b, preferred_element_type=F32)


def dot_nt(a, b):
    return lax.dot_general(a, b, (((1,), (1,)), ((), ())), preferred_element_type=F32)


def dot_tn(a, b):
    return lax.dot_general(a, b, (((0,), (0,)), ((), ())), preferred_element_type=F32)


def cols(*parts):
    return jnp.concatenate(parts, axis=1)


def rows(*parts):
    return jnp.concatenate(parts, axis=0)


def split(pair):
    high = tuple(part.astype(BF16) for part in pair)
    low = tuple((part - top.astype(F32)).astype(BF16) for part, top in zip(pair, high))
    return high, low


def rounded(pair):
    return tuple(part.astype(BF16) for part in pair)


def left_form(pair):
    return cols(pair[0], pair[1])


def right_form(pair):
    return rows(cols(pair[0], pair[1]), cols(-pair[1], pair[0]))


def halves_cols(wide):
    size = wide.shape[1] // 2
    return wide[:, :size], wide[:, size:]


def halves_rows(tall):
    size = tall.shape[0] // 2
    return tall[:size], tall[size:]


def product_one(a, b):
    return halves_cols(dot(left_form(a), right_form(b)))


def product_split(a_high, a_low, b_high, b_low):
    top, right = left_form(a_high), right_form(b_high)
    return halves_cols(
        dot(cols(top, top, left_form(a_low)), rows(right, right_form(b_low), right))
    )


def product(a, b):
    return product_split(*split(a), *split(b))


def product_two(a, b, c):
    a_high, a_low = split(a)
    top, low = left_form(a_high), left_form(a_low)

    def tall(pair):
        high, rest = split(pair)
        right = right_form(high)
        return rows(right, right_form(rest), right)

    both = dot(cols(top, top, low), cols(tall(b), tall(c)))
    size = both.shape[1] // 2
    return halves_cols(both[:, :size]), halves_cols(both[:, size:])


def product_nt(a, b):
    def stacked(pair):
        return rows(cols(pair[0], pair[1]), cols(pair[1], -pair[0]))

    a_high, a_low = split(a)
    b_high, b_low = split(b)
    top, right = stacked(a_high), left_form(b_high)
    return halves_rows(
        dot_nt(cols(top, top, stacked(a_low)), cols(right, left_form(b_low), right))
    )


def product_tn(a, b):
    def tall(pair):
        return rows(pair[0], pair[1])

    def stacked(pair):
        return rows(cols(pair[0], pair[1]), cols(pair[1], -pair[0]))

    a_high, a_low = split(a)
    b_high, b_low = split(b)
    top, right = tall(a_high), stacked(b_high)
    return halves_cols(
        dot_tn(rows(top, top, tall(a_low)), rows(right, stacked(b_low), right))
    )


def minus(a, b):
    return (a[0] - b[0], a[1] - b[1])


def plus(a, b):
    return (a[0] + b[0], a[1] + b[1])


def dagger(a):
    return (a[0].T, -a[1].T)


def load(ref):
    return (ref[0], ref[1])


def save(ref, pair):
    ref[0] = pair[0]
    ref[1] = pair[1]


def square_sum(pair):
    return jnp.sum(pair[0] * pair[0] + pair[1] * pair[1])


def row_col(size):
    shape = (size, size)
    return lax.broadcasted_iota(jnp.int32, shape, 0), lax.broadcasted_iota(jnp.int32, shape, 1)


def identity(size):
    row, col = row_col(size)
    return (row == col).astype(F32)


def pack(pair):
    row, col = row_col(pair[0].shape[0])
    return jnp.where(row > col, pair[0], pair[1])


def unpack(packed):
    row, col = row_col(packed.shape[0])
    flipped = packed.T
    real = jnp.where(row > col, packed, jnp.where(row < col, -flipped, 0.0))
    imag = jnp.where(row > col, flipped, packed)
    return (real, imag)


def scalings():
    low, high, found = 1.0 / POLY_RANGE, 1.0, []
    for _ in range(POLY_STEPS):
        rate = (high - low) / (high + low)
        found.append(2.0 / (low + high))
        low, high = 1.0 - rate * rate, 1.0
    return found


def invert(matrix, out_ref):
    size = matrix[0].shape[0]
    high, low = split(matrix)
    adjoint = dagger(matrix)
    adjoint_16 = rounded(adjoint)
    state = product_one(adjoint_16, high)
    state_16 = rounded(state)
    inverse_bound = NORM_SHARE * lax.rsqrt(square_sum(state))
    both = dot(left_form(state_16), cols(right_form(state_16), right_form(adjoint_16)))
    squared = halves_cols(both[:, : 2 * size])
    moved = halves_cols(both[:, 2 * size :])
    scales = scalings()
    once, twice = 2.0 * scales[0] * inverse_bound, scales[0] ** 2 * inverse_bound**2
    guess = tuple(once * a - twice * q for a, q in zip(adjoint, moved))
    state = tuple(once * s - twice * q for s, q in zip(state, squared))
    for step in range(1, POLY_STEPS):
        once, twice = 2.0 * scales[step], scales[step] ** 2
        state_16, guess_16 = rounded(state), rounded(guess)
        if step < POLY_STEPS - 1:
            both = dot(left_form(state_16), cols(right_form(state_16), right_form(guess_16)))
            squared = halves_cols(both[:, : 2 * size])
            moved = halves_cols(both[:, 2 * size :])
            state = tuple(once * s - twice * q for s, q in zip(state, squared))
        else:
            moved = product_one(state_16, guess_16)
        guess = tuple(once * g - twice * q for g, q in zip(guess, moved))
    guess_high, guess_low = split(guess)
    made = product_split(high, low, guess_high, guess_low)
    residual = (identity(size) - made[0], -made[1])
    residual_16 = rounded(residual)
    second = product_one(residual_16, residual_16)
    fix = product_one(guess_high, rounded(plus(residual, second)))
    save(out_ref, plus(guess, fix))
    good = square_sum(second) < ACCEPT

    @pl.when(jnp.logical_not(good))
    def _():
        square = product(adjoint, matrix)
        bound = jnp.sqrt(square_sum(square))
        save(out_ref, (adjoint[0] / bound, adjoint[1] / bound))

        def more(carry):
            step, left_over = carry
            return jnp.logical_and(step < SLOW_STEPS, jnp.logical_not(left_over < 1e-6))

        def refine(carry):
            step, _ = carry
            now = load(out_ref)
            made = product(matrix, now)
            residual = (identity(size) - made[0], -made[1])
            save(out_ref, plus(now, product(now, residual)))
            return step + 1, square_sum(residual)

        lax.while_loop(more, refine, (jnp.int32(0), jnp.float32(1e30)))


def is_outer():
    place = lax.axis_index("slab")
    return jnp.logical_or(place == 0, place == lax.axis_size("slab") - 1)


def is_inner():
    return jnp.logical_not(is_outer())


def on_left():
    return lax.axis_index("slab") < lax.axis_size("slab") // 2


def bare_matrix(step_width, hamilton, rates):
    size = hamilton[0].shape[-1]
    energy = lax.axis_index("energy").astype(F32) * step_width + EMIN
    eye = identity(size)
    return (energy * eye - hamilton[0], (ETA + rates[...]) * eye - hamilton[1])


def first_kernel(
    step_width, hamilton, couple, lead_left, rates, sigma, fill, send_ref, green_ref, source_ref,
    own_ham, own_lead, own_couple, own_rates, own_sigma, own_green, arrived,
):
    first = lax.axis_index("slab") == 0

    def fetch(source, target, index):
        return pltpu.make_async_copy(source, target, arrived.at[index])

    @pl.when(first)
    def _():
        fetch(lead_left, own_lead, 0).start()

    @pl.when(jnp.logical_not(first))
    def _():
        fetch(couple.at[0], own_lead, 0).start()

    fetch(hamilton.at[0], own_ham, 1).start()
    fetch(rates.at[0], own_rates, 2).start()
    fetch(sigma.at[0, 0], own_sigma, 3).start()

    @pl.when(first)
    def _():
        fetch(couple.at[0], own_couple, 4).start()

    fetch(lead_left, own_lead, 0).wait()
    lead = load(own_lead)
    gamma = product_nt(lead, lead)
    fetch(hamilton.at[0], own_ham, 1).wait()
    fetch(rates.at[0], own_rates, 2).wait()
    real, imag = bare_matrix(step_width, load(own_ham), own_rates)
    fetch(sigma.at[0, 0], own_sigma, 3).wait()
    occupation = jnp.where(first, fill[0, 0], fill[0, 1])
    source_ref[...] = pack(
        (own_sigma[0] - occupation * gamma[1], own_sigma[1] + occupation * gamma[0])
    )
    invert((real - 0.5 * gamma[1], imag + 0.5 * gamma[0]), own_green)
    keep = pltpu.make_async_copy(own_green, green_ref, arrived.at[5])
    keep.start()

    @pl.when(first)
    def _():
        fetch(couple.at[0], own_couple, 4).wait()
        own = load(own_couple)
        right = product_tn(own, load(own_green))
        edge, moved = product_two(right, own, unpack(source_ref[...]))
        save(send_ref, edge)
        send_ref[2] = pack(product_nt(moved, right))

    @pl.when(jnp.logical_not(first))
    def _():
        save(send_ref, load(own_green))
        send_ref[2] = source_ref[...]

    keep.wait()


def outer_less_kernel(couple, green_ref, source_ref, less_ref, across_ref, right_ref):
    green = load(green_ref)
    less = product_nt(product(green, unpack(source_ref[...])), green)
    save(less_ref, less)

    @pl.when(on_left())
    def _():
        own = load(couple.at[0])
        save(across_ref, product(green, own))
        save(right_ref, product_tn(own, less))

    @pl.when(jnp.logical_not(on_left()))
    def _():
        save(across_ref, green)
        save(right_ref, less)


def ready_kernel(step_width, hamilton, rates, couple, matrix_ref, couple_ref):
    save(matrix_ref, bare_matrix(step_width, load(hamilton.at[0]), rates.at[0]))
    save(couple_ref, load(couple.at[0]))


def second_kernel(matrix_in, couple, came, matrix_ref, green_ref, send_ref):
    edge = (came[0], came[1])

    @pl.when(on_left())
    def _():
        save(matrix_ref, minus(load(matrix_in), edge))

    @pl.when(jnp.logical_not(on_left()))
    def _():
        own = load(couple)
        save(matrix_ref, minus(load(matrix_in), product_nt(product(own, edge), own)))

    invert(load(matrix_ref), green_ref)

    @pl.when(on_left())
    def _():
        own = load(couple)
        save(send_ref, product(product_tn(own, load(green_ref)), own))

    @pl.when(jnp.logical_not(on_left()))
    def _():
        save(send_ref, load(green_ref))


def second_less_kernel(sigma, couple, came, green_ref, source_ref, send_ref):
    outside = unpack(came[2])
    own_sigma = (sigma[0, 0, 0], sigma[0, 0, 1])

    @pl.when(on_left())
    def _():
        save(source_ref, plus(own_sigma, outside))

    @pl.when(jnp.logical_not(on_left()))
    def _():
        inside = product(load(couple), (came[0], came[1]))
        save(source_ref, plus(own_sigma, product_nt(product(inside, outside), inside)))

    green = load(green_ref)
    less = product_nt(product(green, load(source_ref)), green)

    @pl.when(on_left())
    def _():
        own = load(couple)
        send_ref[...] = pack(product(product_tn(own, less), own))

    @pl.when(jnp.logical_not(on_left()))
    def _():
        send_ref[...] = pack(less)


def third_kernel(matrix_in, edge, couple, green_ref, send_ref, matrix_ref):
    @pl.when(on_left())
    def _():
        own = load(couple)
        around = product_nt(product(own, load(edge)), own)
        save(matrix_ref, minus(load(matrix_in), around))

    @pl.when(jnp.logical_not(on_left()))
    def _():
        save(matrix_ref, minus(load(matrix_in), load(edge)))

    invert(load(matrix_ref), green_ref)

    @pl.when(on_left())
    def _():
        save(send_ref, load(green_ref))

    @pl.when(jnp.logical_not(on_left()))
    def _():
        own = load(couple)
        save(send_ref, product(product_tn(own, load(green_ref)), own))


def third_less_kernel(source, edge, couple, green_ref, own_ref, send_ref, total_ref):
    came = unpack(edge[...])

    @pl.when(on_left())
    def _():
        own = load(couple)
        save(total_ref, plus(load(source), product_nt(product(own, came), own)))

    @pl.when(jnp.logical_not(on_left()))
    def _():
        save(total_ref, plus(load(source), came))

    green = load(green_ref)
    less = product_nt(product(green, load(total_ref)), green)
    own_ref[...] = pack(less)

    @pl.when(on_left())
    def _():
        send_ref[...] = pack(less)

    @pl.when(jnp.logical_not(on_left()))
    def _():
        own = load(couple)
        send_ref[...] = pack(product(product_tn(own, less), own))


def mixed_kernel(across_ref, right_ref, less_ref, inner_green, base_ref):
    mixed = product(product(load(across_ref), load(inner_green)), load(right_ref))
    save(base_ref, minus(plus(load(less_ref), mixed), dagger(mixed)))


def last_kernel(across_ref, base_ref, inner_less, own_packed, packed_ref, *_):
    across = load(across_ref)
    packed_ref[...] = pack(
        plus(load(base_ref), product_nt(product(across, unpack(inner_less[...])), across))
    )


def message_bits(count, shifts):
    found = {}
    for mode, shift in enumerate(shifts):
        for place in range(count - shift):
            for edge, bit in (((place + shift, place), 0), ((place, place + shift), 1)):
                found[edge] = found.get(edge, 0) | 1 << (2 * mode + bit)
    return found


def coloured(edges, count):
    leaving, coming = [{} for _ in range(count)], [{} for _ in range(count)]
    for source, target in sorted(edges):
        here = min(c for c in range(2 * ROUNDS) if c not in leaving[source])
        there = min(c for c in range(2 * ROUNDS) if c not in coming[target])
        if here != there:
            path, tables, node, colour = [], (coming, leaving), target, here
            side = 0
            while colour in tables[side][node]:
                other = tables[side][node][colour]
                edge = (other, node) if side == 0 else (node, other)
                path.append((edge, colour))
                side, node, colour = 1 - side, other, here + there - colour
            for (start, end), colour in path:
                del leaving[start][colour], coming[end][colour]
            for (start, end), colour in path:
                leaving[start][here + there - colour] = end
                coming[end][here + there - colour] = start
        leaving[source][here] = target
        coming[target][here] = source
    rounds = [[] for _ in range(ROUNDS)]
    for source, table in enumerate(leaving):
        for colour, target in table.items():
            rounds[colour].append((source, target))
    return rounds


def shift_choices():
    return [(a, b) for a in range(1, LARGEST_SHIFT + 1) for b in range(a, LARGEST_SHIFT + 1)]


def choice_of(first, second):
    low = jnp.minimum(first, second) - 1
    high = jnp.maximum(first, second) - 1
    skipped = low * (low + 1)
    skipped = jnp.right_shift(skipped, 1)
    return low * LARGEST_SHIFT - skipped + high


def message_table(count):
    table = []
    for shifts in shift_choices():
        bits = message_bits(count, shifts)
        for pairs in coloured(bits, count):
            row = [0] * count
            for edge in pairs:
                row[edge[1]] = bits[edge]
            table.append(row)
    return np.asarray(table, np.int32).reshape(-1)


def exchange(packed, spare, which):
    count = lax.axis_size("energy")

    def branch_of(shifts):
        rounds = coloured(message_bits(count, shifts), count)

        def branch(block, *spare):
            out = []
            for pairs in rounds:
                out.append(hop(block, "energy", pairs) if pairs else spare[len(out) - 1])
            return tuple(out)

        return branch

    return lax.switch(which, [branch_of(shifts) for shifts in shift_choices()], packed, *spare)


def scatter_kernel(
    table, phonon_fill, phonon_shift, strength, packed, *refs
):
    came, refs = refs[:ROUNDS], refs[ROUNDS:]
    out_ref, lesser_ref, held, sums_ref, own_out, own_lesser, arrived = refs
    count = lax.axis_size("energy")
    which = choice_of(phonon_shift[0], phonon_shift[1])
    swapped = (phonon_shift[0] > phonon_shift[1]).astype(jnp.int32)
    bits = [table[(which * ROUNDS + c) * count + lax.axis_index("energy")] for c in range(ROUNDS)]

    for c in range(ROUNDS):

        @pl.when(bits[c] > 0)
        def _(c=c):
            pltpu.make_async_copy(came[c], held.at[c], arrived.at[c]).start()

    save(own_lesser, unpack(packed[...]))
    give = pltpu.make_async_copy(own_lesser, lesser_ref, arrived.at[ROUNDS])
    give.start()
    sums_ref[...] = jnp.zeros_like(sums_ref)
    for c in range(ROUNDS):

        @pl.when(bits[c] > 0)
        def _(c=c):
            pltpu.make_async_copy(came[c], held.at[c], arrived.at[c]).wait()
            block = held[c]
            for mode in range(2):
                filled = phonon_fill[jnp.where(swapped == 1, 1 - mode, mode)]
                up = (bits[c] // 4**mode % 2).astype(F32)
                down = (bits[c] // (2 * 4**mode) % 2).astype(F32)
                sums_ref[mode] += (up * (filled + 1.0) + down * filled) * block

    near, away = strength[swapped], strength[1 - swapped]
    low, high = unpack(sums_ref[0]), unpack(sums_ref[1])
    done = [pltpu.make_async_copy(own_out.at[p], out_ref.at[p], arrived.at[p]) for p in range(2)]
    for part in range(2):
        own_out[part] = near * low[part] + away * high[part]
        done[part].start()
    for part in range(2):
        done[part].wait()
    give.wait()


def call(body, name, outs, flops, spaces, scratch, active, *args, far_outs=(), pinned=(), aliases=None):
    fetched = [index for index in range(len(args)) if spaces.get(index) is FETCH]
    where = [
        pl.BlockSpec(memory_space=FAR if index in fetched else spaces.get(index, pltpu.VMEM))
        for index in range(len(args))
    ]
    buffers = [pltpu.VMEM(args[index].shape, args[index].dtype) for index in fetched]
    arrivals = [pltpu.SemaphoreType.DMA((len(fetched),))] if fetched else []

    def whole(*refs):
        given, rest = list(refs[: len(args)]), refs[len(args) :]
        own = rest[len(outs) + len(scratch) :]
        rest = rest[: len(outs) + len(scratch)]

        def copies():
            return [
                pltpu.make_async_copy(refs[index], own[slot], own[-1].at[slot])
                for slot, index in enumerate(fetched)
            ]

        def run():
            for copy in copies():
                copy.start()
            for copy in copies():
                copy.wait()
            for slot, index in enumerate(fetched):
                given[index] = own[slot]
            body(*given, *rest)

        if active is None:
            run()
        else:
            pl.when(active())(run)

    made = pl.pallas_call(
        whole,
        out_shape=outs,
        in_specs=where,
        out_specs=[
            pl.BlockSpec(memory_space=FAR if index in far_outs else pltpu.VMEM)
            for index in range(len(outs))
        ],
        scratch_shapes=list(scratch) + buffers + arrivals,
        input_output_aliases=aliases or {},
        compiler_params=pltpu.CompilerParams(vmem_limit_bytes=24 << 20),
        cost_estimate=pl.CostEstimate(flops=flops, bytes_accessed=4 << 20, transcendentals=0),
        name=name,
    )(*[
        pltpu.with_memory_space_constraint(arg, FAR)
        if where[index].memory_space in (FAR, pltpu.SMEM)
        else arg
        for index, arg in enumerate(args)
    ])
    return [
        pltpu.with_memory_space_constraint(out, FAR) if index in pinned else out
        for index, out in enumerate(made)
    ]


def hop(block, axis, pairs):
    return lax.ppermute(block, axis, pairs)


def on_device(
    hamilton, couple, lead_left, rates, fill, sigma_less, strength, phonon_fill, phonon_shift
):
    e_dev, s_dev, _, size, _ = sigma_less.shape
    n_slab = lax.axis_size("slab")
    assert e_dev == 1 and s_dev == 1 and n_slab == 4
    step_width = ESPAN / (e_dev * lax.axis_size("energy"))
    full = jax.ShapeDtypeStruct((2, size, size), F32)
    half = jax.ShapeDtypeStruct((size, size), F32)
    block = pltpu.VMEM((2, size, size), F32)
    inward = [(0, 1), (3, 2)]
    across_middle = [(1, 2), (2, 1)]
    outward = [(1, 0), (2, 3)]
    unit = 24 * size**3

    def first_body(*refs):
        first_kernel(step_width, *refs)

    def ready_body(*refs):
        ready_kernel(step_width, *refs)

    triple = jax.ShapeDtypeStruct((3, size, size), F32)
    which = choice_of(phonon_shift[0], phonon_shift[1])
    sent, green, outer_source = call(
        first_body, "first", [triple, full, half], 11 * unit,
        {**dict.fromkeys(range(5), FAR), 5: pltpu.SMEM},
        [block, block, block, pltpu.VMEM((1, size), F32), block, block, pltpu.SemaphoreType.DMA((6,))],
        is_outer, hamilton, couple, lead_left, rates, sigma_less, fill.T, far_outs=(1,), pinned=(1,),
    )
    came = hop(sent, "slab", inward)
    bare, couple_near = call(
        ready_body, "ready", [full] * 2, unit, dict.fromkeys(range(3), FETCH), [],
        is_inner, hamilton, rates, couple,
    )
    less, across, right = call(
        outer_less_kernel, "outer_less", [full] * 3, 4 * unit, {0: FETCH, 1: FETCH}, [],
        is_outer, couple, green, outer_source,
    )
    came, which, less, across, right = lax.optimization_barrier((came, which, less, across, right))
    matrix, inner_green, sent = call(
        second_kernel, "second", [full] * 3, 10 * unit, {}, [], is_inner, bare, couple_near, came
    )
    edge = hop(sent, "slab", across_middle)
    source, sent = call(
        second_less_kernel, "second_less", [full, half], 6 * unit, {0: FETCH}, [],
        is_inner, sigma_less, couple_near, came, inner_green,
    )
    edge_less = hop(sent, "slab", across_middle)
    edge, sent = lax.optimization_barrier((edge, sent))
    inner_green, sent = call(
        third_kernel, "third", [full] * 2, 8 * unit, {}, [block], is_inner, matrix, edge, couple_near
    )
    came_green = hop(sent, "slab", outward)
    own_packed, sent = call(
        third_less_kernel, "third_less", [half] * 2, 4 * unit, {}, [block],
        is_inner, source, edge_less, couple_near, inner_green,
    )
    came_less = hop(sent, "slab", outward)
    (base,) = call(
        mixed_kernel, "mixed", [full], 2 * unit, {}, [],
        is_outer, across, right, less, came_green,
    )
    packed, *spare = call(
        last_kernel, "last", [half] * ROUNDS, 2 * unit, {}, [],
        is_outer, across, base, came_less, own_packed, far_outs=range(1, ROUNDS), aliases={3: 0},
    )
    around = exchange(packed, spare, which)
    scatter, lesser = call(
        scatter_kernel, "scatter", [full] * 2, unit // 8,
        {0: pltpu.SMEM, 1: pltpu.SMEM, 2: pltpu.SMEM, **dict.fromkeys(range(5, 5 + ROUNDS), FAR)},
        [pltpu.VMEM((ROUNDS, size, size), F32), block, block, block, pltpu.SemaphoreType.DMA((ROUNDS + 1,))],
        None, message_table(lax.axis_size("energy")), phonon_fill, phonon_shift, strength,
        packed, *around, far_outs=(0, 1),
    )
    return (lesser[None, None], scatter[None, None])


def solution(mesh):
    return jax.shard_map(
        on_device,
        mesh=mesh,
        in_specs=(
            P("slab", None, None, None),
            P("slab", None, None, None),
            P(),
            P("energy", "slab", None),
            P(None, "energy"),
            P("energy", "slab", None, None, None),
            P(),
            P(),
            P(),
        ),
        out_specs=(P("energy", "slab", None, None, None), P("energy", "slab", None, None, None)),
        check_vma=False,
    )
```

```python
import jax
import jax.numpy as jnp
import numpy as np
from jax import lax
from jax.experimental import pallas as pl
from jax.experimental.pallas import tpu as pltpu
from jax.sharding import PartitionSpec as P

ETA = 0.2
EMIN = -2.5
ESPAN = 5.0
LARGEST_SHIFT = 6
POLY_STEPS = 5
POLY_RANGE = 90.0
NORM_SHARE = 4.0
ACCEPT = 1e-3
SLOW_STEPS = 80
ROUNDS = 4
FETCH = "fetch"
FAR = pltpu.MemorySpace.HBM

F32 = jnp.float32
BF16 = jnp.bfloat16


def dot(a, b):
    return jnp.dot(a, b, preferred_element_type=F32)


def dot_nt(a, b):
    return lax.dot_general(a, b, (((1,), (1,)), ((), ())), preferred_element_type=F32)


def dot_tn(a, b):
    return lax.dot_general(a, b, (((0,), (0,)), ((), ())), preferred_element_type=F32)


def cols(*parts):
    return jnp.concatenate(parts, axis=1)


def rows(*parts):
    return jnp.concatenate(parts, axis=0)


def split(pair):
    high = tuple(part.astype(BF16) for part in pair)
    low = tuple((part - top.astype(F32)).astype(BF16) for part, top in zip(pair, high))
    return high, low


def rounded(pair):
    return tuple(part.astype(BF16) for part in pair)


def left_form(pair):
    return cols(pair[0], pair[1])


def right_form(pair):
    return rows(cols(pair[0], pair[1]), cols(-pair[1], pair[0]))


def halves_cols(wide):
    size = wide.shape[1] // 2
    return wide[:, :size], wide[:, size:]


def halves_rows(tall):
    size = tall.shape[0] // 2
    return tall[:size], tall[size:]


def product_one(a, b):
    return halves_cols(dot(left_form(a), right_form(b)))


def product_split(a_high, a_low, b_high, b_low):
    top, right = left_form(a_high), right_form(b_high)
    return halves_cols(
        dot(cols(top, top, left_form(a_low)), rows(right, right_form(b_low), right))
    )


def product(a, b):
    return product_split(*split(a), *split(b))


def product_two(a, b, c):
    a_high, a_low = split(a)
    top, low = left_form(a_high), left_form(a_low)

    def tall(pair):
        high, rest = split(pair)
        right = right_form(high)
        return rows(right, right_form(rest), right)

    both = dot(cols(top, top, low), cols(tall(b), tall(c)))
    size = both.shape[1] // 2
    return halves_cols(both[:, :size]), halves_cols(both[:, size:])


def product_nt(a, b):
    def stacked(pair):
        return rows(cols(pair[0], pair[1]), cols(pair[1], -pair[0]))

    a_high, a_low = split(a)
    b_high, b_low = split(b)
    top, right = stacked(a_high), left_form(b_high)
    return halves_rows(
        dot_nt(cols(top, top, stacked(a_low)), cols(right, left_form(b_low), right))
    )


def product_tn(a, b):
    def tall(pair):
        return rows(pair[0], pair[1])

    def stacked(pair):
        return rows(cols(pair[0], pair[1]), cols(pair[1], -pair[0]))

    a_high, a_low = split(a)
    b_high, b_low = split(b)
    top, right = tall(a_high), stacked(b_high)
    return halves_cols(
        dot_tn(rows(top, top, tall(a_low)), rows(right, stacked(b_low), right))
    )


def minus(a, b):
    return (a[0] - b[0], a[1] - b[1])


def plus(a, b):
    return (a[0] + b[0], a[1] + b[1])


def dagger(a):
    return (a[0].T, -a[1].T)


def load(ref):
    return (ref[0], ref[1])


def save(ref, pair):
    ref[0] = pair[0]
    ref[1] = pair[1]


def square_sum(pair):
    return jnp.sum(pair[0] * pair[0] + pair[1] * pair[1])


def row_col(size):
    shape = (size, size)
    return lax.broadcasted_iota(jnp.int32, shape, 0), lax.broadcasted_iota(jnp.int32, shape, 1)


def identity(size):
    row, col = row_col(size)
    return (row == col).astype(F32)


def pack(pair):
    row, col = row_col(pair[0].shape[0])
    return jnp.where(row > col, pair[0], pair[1])


def unpack(packed):
    row, col = row_col(packed.shape[0])
    flipped = packed.T
    real = jnp.where(row > col, packed, jnp.where(row < col, -flipped, 0.0))
    imag = jnp.where(row > col, flipped, packed)
    return (real, imag)


def scalings():
    low, high, found = 1.0 / POLY_RANGE, 1.0, []
    for _ in range(POLY_STEPS):
        rate = (high - low) / (high + low)
        found.append(2.0 / (low + high))
        low, high = 1.0 - rate * rate, 1.0
    return found


def invert(matrix, out_ref):
    size = matrix[0].shape[0]
    high, low = split(matrix)
    adjoint = dagger(matrix)
    adjoint_16 = rounded(adjoint)
    state = product_one(adjoint_16, high)
    state_16 = rounded(state)
    inverse_bound = NORM_SHARE * lax.rsqrt(square_sum(state))
    both = dot(left_form(state_16), cols(right_form(state_16), right_form(adjoint_16)))
    squared = halves_cols(both[:, : 2 * size])
    moved = halves_cols(both[:, 2 * size :])
    scales = scalings()
    once, twice = 2.0 * scales[0] * inverse_bound, scales[0] ** 2 * inverse_bound**2
    guess = tuple(once * a - twice * q for a, q in zip(adjoint, moved))
    state = tuple(once * s - twice * q for s, q in zip(state, squared))
    for step in range(1, POLY_STEPS):
        once, twice = 2.0 * scales[step], scales[step] ** 2
        state_16, guess_16 = rounded(state), rounded(guess)
        if step < POLY_STEPS - 1:
            both = dot(left_form(state_16), cols(right_form(state_16), right_form(guess_16)))
            squared = halves_cols(both[:, : 2 * size])
            moved = halves_cols(both[:, 2 * size :])
            state = tuple(once * s - twice * q for s, q in zip(state, squared))
        else:
            moved = product_one(state_16, guess_16)
        guess = tuple(once * g - twice * q for g, q in zip(guess, moved))
    guess_high, guess_low = split(guess)
    made = product_split(high, low, guess_high, guess_low)
    residual = (identity(size) - made[0], -made[1])
    residual_16 = rounded(residual)
    second = product_one(residual_16, residual_16)
    fix = product_one(guess_high, rounded(plus(residual, second)))
    save(out_ref, plus(guess, fix))
    good = square_sum(second) < ACCEPT

    @pl.when(jnp.logical_not(good))
    def _():
        square = product(adjoint, matrix)
        bound = jnp.sqrt(square_sum(square))
        save(out_ref, (adjoint[0] / bound, adjoint[1] / bound))

        def more(carry):
            step, left_over = carry
            return jnp.logical_and(step < SLOW_STEPS, jnp.logical_not(left_over < 1e-6))

        def refine(carry):
            step, _ = carry
            now = load(out_ref)
            made = product(matrix, now)
            residual = (identity(size) - made[0], -made[1])
            save(out_ref, plus(now, product(now, residual)))
            return step + 1, square_sum(residual)

        lax.while_loop(more, refine, (jnp.int32(0), jnp.float32(1e30)))


def is_outer():
    place = lax.axis_index("slab")
    return jnp.logical_or(place == 0, place == lax.axis_size("slab") - 1)


def is_inner():
    return jnp.logical_not(is_outer())


def on_left():
    return lax.axis_index("slab") < lax.axis_size("slab") // 2


def bare_matrix(step_width, hamilton, rates):
    size = hamilton[0].shape[-1]
    energy = lax.axis_index("energy").astype(F32) * step_width + EMIN
    eye = identity(size)
    return (energy * eye - hamilton[0], (ETA + rates[...]) * eye - hamilton[1])


def choose_kernel(phonon_shift, which):
    which[0] = choice_of(phonon_shift[0], phonon_shift[1])


def first_kernel(
    step_width, hamilton, couple, lead_left, rates, sigma, fill, send_ref, green_ref, source_ref,
    own_ham, own_lead, own_couple, own_rates, own_sigma, own_green, arrived,
):
    first = lax.axis_index("slab") == 0

    def fetch(source, target, index):
        return pltpu.make_async_copy(source, target, arrived.at[index])

    @pl.when(first)
    def _():
        fetch(lead_left, own_lead, 0).start()

    @pl.when(jnp.logical_not(first))
    def _():
        fetch(couple.at[0], own_lead, 0).start()

    fetch(hamilton.at[0], own_ham, 1).start()
    fetch(rates.at[0], own_rates, 2).start()
    fetch(sigma.at[0, 0], own_sigma, 3).start()

    @pl.when(first)
    def _():
        fetch(couple.at[0], own_couple, 4).start()

    fetch(lead_left, own_lead, 0).wait()
    lead = load(own_lead)
    gamma = product_nt(lead, lead)
    fetch(hamilton.at[0], own_ham, 1).wait()
    fetch(rates.at[0], own_rates, 2).wait()
    real, imag = bare_matrix(step_width, load(own_ham), own_rates)
    fetch(sigma.at[0, 0], own_sigma, 3).wait()
    occupation = jnp.where(first, fill[0, 0], fill[0, 1])
    source_ref[...] = pack(
        (own_sigma[0] - occupation * gamma[1], own_sigma[1] + occupation * gamma[0])
    )
    invert((real - 0.5 * gamma[1], imag + 0.5 * gamma[0]), own_green)
    save(green_ref, load(own_green))

    @pl.when(first)
    def _():
        fetch(couple.at[0], own_couple, 4).wait()
        own = load(own_couple)
        right = product_tn(own, load(own_green))
        edge, moved = product_two(right, own, unpack(source_ref[...]))
        save(send_ref, edge)
        send_ref[2] = pack(product_nt(moved, right))

    @pl.when(jnp.logical_not(first))
    def _():
        save(send_ref, load(own_green))
        send_ref[2] = source_ref[...]


def outer_less_kernel(couple, green_ref, source_ref, less_ref, across_ref, right_ref):
    green = load(green_ref)
    less = product_nt(product(green, unpack(source_ref[...])), green)
    save(less_ref, less)

    @pl.when(on_left())
    def _():
        own = load(couple.at[0])
        save(across_ref, product(green, own))
        save(right_ref, product_tn(own, less))

    @pl.when(jnp.logical_not(on_left()))
    def _():
        save(across_ref, green)
        save(right_ref, less)


def ready_kernel(step_width, hamilton, rates, couple, matrix_ref, couple_ref):
    save(matrix_ref, bare_matrix(step_width, load(hamilton.at[0]), rates.at[0]))
    save(couple_ref, load(couple.at[0]))


def second_kernel(matrix_in, couple, came, matrix_ref, green_ref, send_ref):
    edge = (came[0], came[1])

    @pl.when(on_left())
    def _():
        save(matrix_ref, minus(load(matrix_in), edge))

    @pl.when(jnp.logical_not(on_left()))
    def _():
        own = load(couple)
        save(matrix_ref, minus(load(matrix_in), product_nt(product(own, edge), own)))

    invert(load(matrix_ref), green_ref)

    @pl.when(on_left())
    def _():
        own = load(couple)
        save(send_ref, product(product_tn(own, load(green_ref)), own))

    @pl.when(jnp.logical_not(on_left()))
    def _():
        save(send_ref, load(green_ref))


def second_less_kernel(sigma, couple, came, green_ref, source_ref, send_ref):
    outside = unpack(came[2])
    own_sigma = (sigma[0, 0, 0], sigma[0, 0, 1])

    @pl.when(on_left())
    def _():
        save(source_ref, plus(own_sigma, outside))

    @pl.when(jnp.logical_not(on_left()))
    def _():
        inside = product(load(couple), (came[0], came[1]))
        save(source_ref, plus(own_sigma, product_nt(product(inside, outside), inside)))

    green = load(green_ref)
    less = product_nt(product(green, load(source_ref)), green)

    @pl.when(on_left())
    def _():
        own = load(couple)
        send_ref[...] = pack(product(product_tn(own, less), own))

    @pl.when(jnp.logical_not(on_left()))
    def _():
        send_ref[...] = pack(less)


def third_kernel(matrix_in, edge, couple, green_ref, send_ref, matrix_ref):
    @pl.when(on_left())
    def _():
        own = load(couple)
        around = product_nt(product(own, load(edge)), own)
        save(matrix_ref, minus(load(matrix_in), around))

    @pl.when(jnp.logical_not(on_left()))
    def _():
        save(matrix_ref, minus(load(matrix_in), load(edge)))

    invert(load(matrix_ref), green_ref)

    @pl.when(on_left())
    def _():
        save(send_ref, load(green_ref))

    @pl.when(jnp.logical_not(on_left()))
    def _():
        own = load(couple)
        save(send_ref, product(product_tn(own, load(green_ref)), own))


def third_less_kernel(source, edge, couple, green_ref, own_ref, send_ref, total_ref):
    came = unpack(edge[...])

    @pl.when(on_left())
    def _():
        own = load(couple)
        save(total_ref, plus(load(source), product_nt(product(own, came), own)))

    @pl.when(jnp.logical_not(on_left()))
    def _():
        save(total_ref, plus(load(source), came))

    green = load(green_ref)
    less = product_nt(product(green, load(total_ref)), green)
    own_ref[...] = pack(less)

    @pl.when(on_left())
    def _():
        send_ref[...] = pack(less)

    @pl.when(jnp.logical_not(on_left()))
    def _():
        own = load(couple)
        send_ref[...] = pack(product(product_tn(own, less), own))


def mixed_kernel(across_ref, right_ref, less_ref, inner_green, base_ref):
    mixed = product(product(load(across_ref), load(inner_green)), load(right_ref))
    save(base_ref, minus(plus(load(less_ref), mixed), dagger(mixed)))


def last_kernel(across_ref, base_ref, inner_less, own_packed, packed_ref, *_):
    across = load(across_ref)
    packed_ref[...] = pack(
        plus(load(base_ref), product_nt(product(across, unpack(inner_less[...])), across))
    )


def message_bits(count, shifts):
    found = {}
    for mode, shift in enumerate(shifts):
        for place in range(count - shift):
            for edge, bit in (((place + shift, place), 0), ((place, place + shift), 1)):
                found[edge] = found.get(edge, 0) | 1 << (2 * mode + bit)
    return found


def rounds_of(count, shifts):
    moves = []
    for shift in sorted(set(shifts)):
        moves.append([(place + shift, place) for place in range(count - shift)])
        moves.append([(place, place + shift) for place in range(count - shift)])

    def fits(pairs, more):
        return all({p[end] for p in pairs}.isdisjoint({p[end] for p in more}) for end in range(2))

    def placed(index, rounds):
        if index == len(moves):
            return rounds
        found = [
            placed(index + 1, rounds[:r] + [rounds[r] + moves[index]] + rounds[r + 1 :])
            for r in range(len(rounds))
            if fits(rounds[r], moves[index])
        ]
        found.append(placed(index + 1, rounds + [moves[index]]))
        return min(found, key=len)

    best = placed(0, [])
    return best + [[]] * (ROUNDS - len(best))


def shift_choices():
    return [(a, b) for a in range(1, LARGEST_SHIFT + 1) for b in range(a, LARGEST_SHIFT + 1)]


def choice_of(first, second):
    low = jnp.minimum(first, second) - 1
    high = jnp.maximum(first, second) - 1
    skipped = low * (low + 1)
    skipped = jnp.right_shift(skipped, 1)
    return low * LARGEST_SHIFT - skipped + high


def message_table(count):
    table = []
    for shifts in shift_choices():
        bits = message_bits(count, shifts)
        for pairs in rounds_of(count, shifts):
            row = [0] * count
            for edge in pairs:
                row[edge[1]] = bits[edge]
            table.append(row)
    return np.asarray(table, np.int32).reshape(-1)


def finish_kernel(packed, lesser_ref):
    save(lesser_ref, unpack(packed[...]))


def exchange(packed, spare, which):
    count, size = lax.axis_size("energy"), packed.shape[-1]

    def branch_of(shifts):
        rounds = rounds_of(count, shifts)

        def branch(block, *spare):
            out = []
            for pairs in rounds:
                out.append(hop(block, "energy", pairs) if pairs else spare[len(out) - 1])
            (lesser,) = call(
                finish_kernel, "finish", [jax.ShapeDtypeStruct((2, size, size), F32)], 64 * size**3,
                {}, [], None, block,
            )
            return (*out, lesser)

        return branch

    return lax.switch(which, [branch_of(shifts) for shifts in shift_choices()], packed, *spare)


def scatter_kernel(
    table, phonon_fill, phonon_shift, strength, *refs
):
    came, refs = refs[:ROUNDS], refs[ROUNDS:]
    out_ref, held, sums_ref, own_out, arrived = refs
    count = lax.axis_size("energy")
    which = choice_of(phonon_shift[0], phonon_shift[1])
    swapped = (phonon_shift[0] > phonon_shift[1]).astype(jnp.int32)
    bits = [table[(which * ROUNDS + c) * count + lax.axis_index("energy")] for c in range(ROUNDS)]

    for c in range(ROUNDS):

        @pl.when(bits[c] > 0)
        def _(c=c):
            pltpu.make_async_copy(came[c], held.at[c], arrived.at[c]).start()

    sums_ref[...] = jnp.zeros_like(sums_ref)
    for c in range(ROUNDS):

        @pl.when(bits[c] > 0)
        def _(c=c):
            pltpu.make_async_copy(came[c], held.at[c], arrived.at[c]).wait()
            block = held[c]
            for mode in range(2):
                filled = phonon_fill[jnp.where(swapped == 1, 1 - mode, mode)]
                up = (bits[c] // 4**mode % 2).astype(F32)
                down = (bits[c] // (2 * 4**mode) % 2).astype(F32)
                sums_ref[mode] += (up * (filled + 1.0) + down * filled) * block

    near, away = strength[swapped], strength[1 - swapped]
    low, high = unpack(sums_ref[0]), unpack(sums_ref[1])
    done = [pltpu.make_async_copy(own_out.at[p], out_ref.at[p], arrived.at[p]) for p in range(2)]
    for part in range(2):
        own_out[part] = near * low[part] + away * high[part]
        done[part].start()
    for part in range(2):
        done[part].wait()


def call(body, name, outs, flops, spaces, scratch, active, *args, far_outs=(), small_outs=(), aliases=None):
    fetched = [index for index in range(len(args)) if spaces.get(index) is FETCH]
    where = [
        pl.BlockSpec(memory_space=FAR if index in fetched else spaces.get(index, pltpu.VMEM))
        for index in range(len(args))
    ]
    buffers = [pltpu.VMEM(args[index].shape, args[index].dtype) for index in fetched]
    arrivals = [pltpu.SemaphoreType.DMA((len(fetched),))] if fetched else []

    def whole(*refs):
        given, rest = list(refs[: len(args)]), refs[len(args) :]
        own = rest[len(outs) + len(scratch) :]
        rest = rest[: len(outs) + len(scratch)]

        def copies():
            return [
                pltpu.make_async_copy(refs[index], own[slot], own[-1].at[slot])
                for slot, index in enumerate(fetched)
            ]

        def run():
            for copy in copies():
                copy.start()
            for copy in copies():
                copy.wait()
            for slot, index in enumerate(fetched):
                given[index] = own[slot]
            body(*given, *rest)

        if active is None:
            run()
        else:
            pl.when(active())(run)

    made = pl.pallas_call(
        whole,
        out_shape=outs,
        in_specs=where,
        out_specs=[
            pl.BlockSpec(
                memory_space=FAR if index in far_outs else pltpu.SMEM if index in small_outs else pltpu.VMEM
            )
            for index in range(len(outs))
        ],
        scratch_shapes=list(scratch) + buffers + arrivals,
        input_output_aliases=aliases or {},
        compiler_params=pltpu.CompilerParams(vmem_limit_bytes=24 << 20),
        cost_estimate=pl.CostEstimate(flops=flops, bytes_accessed=4 << 20, transcendentals=0),
        name=name,
    )(*[
        pltpu.with_memory_space_constraint(arg, FAR)
        if where[index].memory_space in (FAR, pltpu.SMEM)
        else arg
        for index, arg in enumerate(args)
    ])
    return made


def hop(block, axis, pairs):
    return lax.ppermute(block, axis, pairs)


def on_device(
    hamilton, couple, lead_left, rates, fill, sigma_less, strength, phonon_fill, phonon_shift
):
    e_dev, s_dev, _, size, _ = sigma_less.shape
    n_slab = lax.axis_size("slab")
    assert e_dev == 1 and s_dev == 1 and n_slab == 4
    step_width = ESPAN / (e_dev * lax.axis_size("energy"))
    full = jax.ShapeDtypeStruct((2, size, size), F32)
    half = jax.ShapeDtypeStruct((size, size), F32)
    block = pltpu.VMEM((2, size, size), F32)
    inward = [(0, 1), (3, 2)]
    across_middle = [(1, 2), (2, 1)]
    outward = [(1, 0), (2, 3)]
    unit = 24 * size**3

    def first_body(*refs):
        first_kernel(step_width, *refs)

    def ready_body(*refs):
        ready_kernel(step_width, *refs)

    triple = jax.ShapeDtypeStruct((3, size, size), F32)
    (which,) = call(
        choose_kernel, "choose", [jax.ShapeDtypeStruct((1,), jnp.int32)], 8, {0: pltpu.SMEM}, [],
        None, phonon_shift, small_outs=(0,),
    )
    sent, green, outer_source = call(
        first_body, "first", [triple, full, half], 11 * unit,
        {**dict.fromkeys(range(5), FAR), 5: pltpu.SMEM},
        [block, block, block, pltpu.VMEM((1, size), F32), block, block, pltpu.SemaphoreType.DMA((6,))],
        is_outer, hamilton, couple, lead_left, rates, sigma_less, fill.T,
    )
    came = hop(sent, "slab", inward)
    bare, couple_near = call(
        ready_body, "ready", [full] * 2, unit, dict.fromkeys(range(3), FETCH), [],
        is_inner, hamilton, rates, couple,
    )
    less, across, right = call(
        outer_less_kernel, "outer_less", [full] * 3, 4 * unit, {0: FETCH}, [],
        is_outer, couple, green, outer_source,
    )
    came, which = lax.optimization_barrier((came, which))
    matrix, inner_green, sent = call(
        second_kernel, "second", [full] * 3, 10 * unit, {}, [], is_inner, bare, couple_near, came
    )
    edge = hop(sent, "slab", across_middle)
    source, sent = call(
        second_less_kernel, "second_less", [full, half], 6 * unit, {0: FETCH}, [],
        is_inner, sigma_less, couple_near, came, inner_green,
    )
    edge_less = hop(sent, "slab", across_middle)
    edge, sent = lax.optimization_barrier((edge, sent))
    inner_green, sent = call(
        third_kernel, "third", [full] * 2, 8 * unit, {}, [block], is_inner, matrix, edge, couple_near
    )
    came_green = hop(sent, "slab", outward)
    own_packed, sent = call(
        third_less_kernel, "third_less", [half] * 2, 4 * unit, {}, [block],
        is_inner, source, edge_less, couple_near, inner_green,
    )
    came_less = hop(sent, "slab", outward)
    (base,) = call(
        mixed_kernel, "mixed", [full], 2 * unit, {}, [],
        is_outer, across, right, less, came_green,
    )
    packed, *spare = call(
        last_kernel, "last", [half] * ROUNDS, 2 * unit, {}, [],
        is_outer, across, base, came_less, own_packed, far_outs=range(1, ROUNDS), aliases={3: 0},
    )
    *around, lesser = exchange(packed, spare, which[0])
    (scatter,) = call(
        scatter_kernel, "scatter", [full], unit // 8,
        {0: pltpu.SMEM, 1: pltpu.SMEM, 2: pltpu.SMEM, **dict.fromkeys(range(4, 4 + ROUNDS), FAR)},
        [pltpu.VMEM((ROUNDS, size, size), F32), block, block, pltpu.SemaphoreType.DMA((ROUNDS,))],
        None, message_table(lax.axis_size("energy")), phonon_fill, phonon_shift, strength,
        *around, far_outs=(0,),
    )
    return (lesser[None, None], scatter[None, None])


def solution(mesh):
    return jax.shard_map(
        on_device,
        mesh=mesh,
        in_specs=(
            P("slab", None, None, None),
            P("slab", None, None, None),
            P(),
            P("energy", "slab", None),
            P(None, "energy"),
            P("energy", "slab", None, None, None),
            P(),
            P(),
            P(),
        ),
        out_specs=(P("energy", "slab", None, None, None), P("energy", "slab", None, None, None)),
        check_vma=False,
    )
```

```python
import jax
import jax.numpy as jnp
import numpy as np
from jax import lax
from jax.experimental import pallas as pl
from jax.experimental.pallas import tpu as pltpu
from jax.sharding import PartitionSpec as P

ETA = 0.2
EMIN = -2.5
ESPAN = 5.0
LARGEST_SHIFT = 6
POLY_STEPS = 5
POLY_RANGE = 90.0
NORM_SHARE = 4.0
ACCEPT = 1e-3
SLOW_STEPS = 80
ROUNDS = 4
FETCH = "fetch"
FAR = pltpu.MemorySpace.HBM

F32 = jnp.float32
BF16 = jnp.bfloat16


def dot(a, b):
    return jnp.dot(a, b, preferred_element_type=F32)


def dot_nt(a, b):
    return lax.dot_general(a, b, (((1,), (1,)), ((), ())), preferred_element_type=F32)


def dot_tn(a, b):
    return lax.dot_general(a, b, (((0,), (0,)), ((), ())), preferred_element_type=F32)


def cols(*parts):
    return jnp.concatenate(parts, axis=1)


def rows(*parts):
    return jnp.concatenate(parts, axis=0)


def split(pair):
    high = tuple(part.astype(BF16) for part in pair)
    low = tuple((part - top.astype(F32)).astype(BF16) for part, top in zip(pair, high))
    return high, low


def rounded(pair):
    return tuple(part.astype(BF16) for part in pair)


def left_form(pair):
    return cols(pair[0], pair[1])


def right_form(pair):
    return rows(cols(pair[0], pair[1]), cols(-pair[1], pair[0]))


def halves_cols(wide):
    size = wide.shape[1] // 2
    return wide[:, :size], wide[:, size:]


def halves_rows(tall):
    size = tall.shape[0] // 2
    return tall[:size], tall[size:]


def product_one(a, b):
    return halves_cols(dot(left_form(a), right_form(b)))


def product_split(a_high, a_low, b_high, b_low):
    top, right = left_form(a_high), right_form(b_high)
    return halves_cols(
        dot(cols(top, top, left_form(a_low)), rows(right, right_form(b_low), right))
    )


def product(a, b):
    return product_split(*split(a), *split(b))


def product_two(a, b, c):
    a_high, a_low = split(a)
    top, low = left_form(a_high), left_form(a_low)

    def tall(pair):
        high, rest = split(pair)
        right = right_form(high)
        return rows(right, right_form(rest), right)

    both = dot(cols(top, top, low), cols(tall(b), tall(c)))
    size = both.shape[1] // 2
    return halves_cols(both[:, :size]), halves_cols(both[:, size:])


def product_nt(a, b):
    def stacked(pair):
        return rows(cols(pair[0], pair[1]), cols(pair[1], -pair[0]))

    a_high, a_low = split(a)
    b_high, b_low = split(b)
    top, right = stacked(a_high), left_form(b_high)
    return halves_rows(
        dot_nt(cols(top, top, stacked(a_low)), cols(right, left_form(b_low), right))
    )


def product_tn(a, b):
    def tall(pair):
        return rows(pair[0], pair[1])

    def stacked(pair):
        return rows(cols(pair[0], pair[1]), cols(pair[1], -pair[0]))

    a_high, a_low = split(a)
    b_high, b_low = split(b)
    top, right = tall(a_high), stacked(b_high)
    return halves_cols(
        dot_tn(rows(top, top, tall(a_low)), rows(right, stacked(b_low), right))
    )


def minus(a, b):
    return (a[0] - b[0], a[1] - b[1])


def plus(a, b):
    return (a[0] + b[0], a[1] + b[1])


def dagger(a):
    return (a[0].T, -a[1].T)


def load(ref):
    return (ref[0], ref[1])


def save(ref, pair):
    ref[0] = pair[0]
    ref[1] = pair[1]


def square_sum(pair):
    return jnp.sum(pair[0] * pair[0] + pair[1] * pair[1])


def row_col(size):
    shape = (size, size)
    return lax.broadcasted_iota(jnp.int32, shape, 0), lax.broadcasted_iota(jnp.int32, shape, 1)


def identity(size):
    row, col = row_col(size)
    return (row == col).astype(F32)


def pack(pair):
    row, col = row_col(pair[0].shape[0])
    return jnp.where(row > col, pair[0], pair[1])


def unpack(packed):
    row, col = row_col(packed.shape[0])
    flipped = packed.T
    real = jnp.where(row > col, packed, jnp.where(row < col, -flipped, 0.0))
    imag = jnp.where(row > col, flipped, packed)
    return (real, imag)


def scalings():
    low, high, found = 1.0 / POLY_RANGE, 1.0, []
    for _ in range(POLY_STEPS):
        rate = (high - low) / (high + low)
        found.append(2.0 / (low + high))
        low, high = 1.0 - rate * rate, 1.0
    return found


def invert(matrix, out_ref):
    size = matrix[0].shape[0]
    high, low = split(matrix)
    adjoint = dagger(matrix)
    adjoint_16 = rounded(adjoint)
    state = product_one(adjoint_16, high)
    state_16 = rounded(state)
    inverse_bound = NORM_SHARE * lax.rsqrt(square_sum(state))
    both = dot(left_form(state_16), cols(right_form(state_16), right_form(adjoint_16)))
    squared = halves_cols(both[:, : 2 * size])
    moved = halves_cols(both[:, 2 * size :])
    scales = scalings()
    once, twice = 2.0 * scales[0] * inverse_bound, scales[0] ** 2 * inverse_bound**2
    guess = tuple(once * a - twice * q for a, q in zip(adjoint, moved))
    state = tuple(once * s - twice * q for s, q in zip(state, squared))
    for step in range(1, POLY_STEPS):
        once, twice = 2.0 * scales[step], scales[step] ** 2
        state_16, guess_16 = rounded(state), rounded(guess)
        if step < POLY_STEPS - 1:
            both = dot(left_form(state_16), cols(right_form(state_16), right_form(guess_16)))
            squared = halves_cols(both[:, : 2 * size])
            moved = halves_cols(both[:, 2 * size :])
            state = tuple(once * s - twice * q for s, q in zip(state, squared))
        else:
            moved = product_one(state_16, guess_16)
        guess = tuple(once * g - twice * q for g, q in zip(guess, moved))
    guess_high, guess_low = split(guess)
    made = product_split(high, low, guess_high, guess_low)
    residual = (identity(size) - made[0], -made[1])
    residual_16 = rounded(residual)
    second = product_one(residual_16, residual_16)
    fix = product_one(guess_high, rounded(plus(residual, second)))
    save(out_ref, plus(guess, fix))
    good = square_sum(second) < ACCEPT

    @pl.when(jnp.logical_not(good))
    def _():
        square = product(adjoint, matrix)
        bound = jnp.sqrt(square_sum(square))
        save(out_ref, (adjoint[0] / bound, adjoint[1] / bound))

        def more(carry):
            step, left_over = carry
            return jnp.logical_and(step < SLOW_STEPS, jnp.logical_not(left_over < 1e-6))

        def refine(carry):
            step, _ = carry
            now = load(out_ref)
            made = product(matrix, now)
            residual = (identity(size) - made[0], -made[1])
            save(out_ref, plus(now, product(now, residual)))
            return step + 1, square_sum(residual)

        lax.while_loop(more, refine, (jnp.int32(0), jnp.float32(1e30)))


def is_outer():
    place = lax.axis_index("slab")
    return jnp.logical_or(place == 0, place == lax.axis_size("slab") - 1)


def is_inner():
    return jnp.logical_not(is_outer())


def on_left():
    return lax.axis_index("slab") < lax.axis_size("slab") // 2


def bare_matrix(step_width, hamilton, rates):
    size = hamilton[0].shape[-1]
    energy = lax.axis_index("energy").astype(F32) * step_width + EMIN
    eye = identity(size)
    return (energy * eye - hamilton[0], (ETA + rates[...]) * eye - hamilton[1])


def choose_kernel(phonon_shift, which):
    which[0] = choice_of(phonon_shift[0], phonon_shift[1])


def first_kernel(
    step_width, hamilton, couple, lead_left, rates, sigma, fill, send_ref, green_ref, source_ref,
    own_ham, own_lead, own_couple, own_rates, own_sigma, own_green, arrived,
):
    first = lax.axis_index("slab") == 0

    def fetch(source, target, index):
        return pltpu.make_async_copy(source, target, arrived.at[index])

    @pl.when(first)
    def _():
        fetch(lead_left, own_lead, 0).start()

    @pl.when(jnp.logical_not(first))
    def _():
        fetch(couple.at[0], own_lead, 0).start()

    fetch(rates.at[0], own_rates, 2).start()
    fetch(hamilton.at[0], own_ham, 1).start()
    fetch(lead_left, own_lead, 0).wait()
    fetch(sigma.at[0, 0], own_sigma, 3).start()

    @pl.when(first)
    def _():
        fetch(couple.at[0], own_couple, 4).start()

    lead = load(own_lead)
    gamma = product_nt(lead, lead)
    fetch(hamilton.at[0], own_ham, 1).wait()
    fetch(rates.at[0], own_rates, 2).wait()
    real, imag = bare_matrix(step_width, load(own_ham), own_rates)
    save(own_lead, gamma)
    invert((real - 0.5 * gamma[1], imag + 0.5 * gamma[0]), own_green)
    save(green_ref, load(own_green))
    fetch(sigma.at[0, 0], own_sigma, 3).wait()
    occupation = jnp.where(first, fill[0, 0], fill[0, 1])
    save(
        own_sigma, (own_sigma[0] - occupation * own_lead[1], own_sigma[1] + occupation * own_lead[0])
    )
    source_ref[...] = pack(load(own_sigma))

    @pl.when(first)
    def _():
        fetch(couple.at[0], own_couple, 4).wait()
        own = load(own_couple)
        right = product_tn(own, load(own_green))
        edge, moved = product_two(right, own, load(own_sigma))
        save(send_ref, edge)
        send_ref[2] = pack(product_nt(moved, right))

    @pl.when(jnp.logical_not(first))
    def _():
        save(send_ref, load(own_green))
        send_ref[2] = source_ref[...]


def outer_less_kernel(couple, green_ref, source_ref, less_ref, across_ref, right_ref):
    green = load(green_ref)
    less = product_nt(product(green, unpack(source_ref[...])), green)
    save(less_ref, less)

    @pl.when(on_left())
    def _():
        own = load(couple.at[0])
        save(across_ref, product(green, own))
        save(right_ref, product_tn(own, less))

    @pl.when(jnp.logical_not(on_left()))
    def _():
        save(across_ref, green)
        save(right_ref, less)


def ready_kernel(step_width, hamilton, rates, couple, matrix_ref, couple_ref):
    save(matrix_ref, bare_matrix(step_width, load(hamilton.at[0]), rates.at[0]))
    save(couple_ref, load(couple.at[0]))


def second_kernel(matrix_in, couple, came, matrix_ref, green_ref, send_ref):
    edge = (came[0], came[1])

    @pl.when(on_left())
    def _():
        save(matrix_ref, minus(load(matrix_in), edge))

    @pl.when(jnp.logical_not(on_left()))
    def _():
        own = load(couple)
        save(matrix_ref, minus(load(matrix_in), product_nt(product(own, edge), own)))

    invert(load(matrix_ref), green_ref)

    @pl.when(on_left())
    def _():
        own = load(couple)
        save(send_ref, product(product_tn(own, load(green_ref)), own))

    @pl.when(jnp.logical_not(on_left()))
    def _():
        save(send_ref, load(green_ref))


def second_less_kernel(sigma, couple, came, green_ref, source_ref, send_ref):
    outside = unpack(came[2])
    own_sigma = (sigma[0, 0, 0], sigma[0, 0, 1])

    @pl.when(on_left())
    def _():
        save(source_ref, plus(own_sigma, outside))

    @pl.when(jnp.logical_not(on_left()))
    def _():
        inside = product(load(couple), (came[0], came[1]))
        save(source_ref, plus(own_sigma, product_nt(product(inside, outside), inside)))

    green = load(green_ref)
    less = product_nt(product(green, load(source_ref)), green)

    @pl.when(on_left())
    def _():
        own = load(couple)
        send_ref[...] = pack(product(product_tn(own, less), own))

    @pl.when(jnp.logical_not(on_left()))
    def _():
        send_ref[...] = pack(less)


def third_kernel(matrix_in, edge, couple, green_ref, send_ref, matrix_ref):
    @pl.when(on_left())
    def _():
        own = load(couple)
        around = product_nt(product(own, load(edge)), own)
        save(matrix_ref, minus(load(matrix_in), around))

    @pl.when(jnp.logical_not(on_left()))
    def _():
        save(matrix_ref, minus(load(matrix_in), load(edge)))

    invert(load(matrix_ref), green_ref)

    @pl.when(on_left())
    def _():
        save(send_ref, load(green_ref))

    @pl.when(jnp.logical_not(on_left()))
    def _():
        own = load(couple)
        save(send_ref, product(product_tn(own, load(green_ref)), own))


def third_less_kernel(source, edge, couple, green_ref, own_ref, send_ref, total_ref):
    came = unpack(edge[...])

    @pl.when(on_left())
    def _():
        own = load(couple)
        save(total_ref, plus(load(source), product_nt(product(own, came), own)))

    @pl.when(jnp.logical_not(on_left()))
    def _():
        save(total_ref, plus(load(source), came))

    green = load(green_ref)
    less = product_nt(product(green, load(total_ref)), green)
    own_ref[...] = pack(less)

    @pl.when(on_left())
    def _():
        send_ref[...] = pack(less)

    @pl.when(jnp.logical_not(on_left()))
    def _():
        own = load(couple)
        send_ref[...] = pack(product(product_tn(own, less), own))


def mixed_kernel(across_ref, right_ref, less_ref, inner_green, base_ref):
    mixed = product(product(load(across_ref), load(inner_green)), load(right_ref))
    save(base_ref, minus(plus(load(less_ref), mixed), dagger(mixed)))


def last_kernel(across_ref, base_ref, inner_less, own_packed, packed_ref, *_):
    across = load(across_ref)
    packed_ref[...] = pack(
        plus(load(base_ref), product_nt(product(across, unpack(inner_less[...])), across))
    )


def message_bits(count, shifts):
    found = {}
    for mode, shift in enumerate(shifts):
        for place in range(count - shift):
            for edge, bit in (((place + shift, place), 0), ((place, place + shift), 1)):
                found[edge] = found.get(edge, 0) | 1 << (2 * mode + bit)
    return found


def rounds_of(count, shifts):
    moves = []
    for shift in sorted(set(shifts)):
        moves.append([(place + shift, place) for place in range(count - shift)])
        moves.append([(place, place + shift) for place in range(count - shift)])

    def fits(pairs, more):
        return all({p[end] for p in pairs}.isdisjoint({p[end] for p in more}) for end in range(2))

    def placed(index, rounds):
        if index == len(moves):
            return rounds
        found = [
            placed(index + 1, rounds[:r] + [rounds[r] + moves[index]] + rounds[r + 1 :])
            for r in range(len(rounds))
            if fits(rounds[r], moves[index])
        ]
        found.append(placed(index + 1, rounds + [moves[index]]))
        return min(found, key=len)

    best = placed(0, [])
    return best + [[]] * (ROUNDS - len(best))


def shift_choices():
    return [(a, b) for a in range(1, LARGEST_SHIFT + 1) for b in range(a, LARGEST_SHIFT + 1)]


def choice_of(first, second):
    low = jnp.minimum(first, second) - 1
    high = jnp.maximum(first, second) - 1
    skipped = low * (low + 1)
    skipped = jnp.right_shift(skipped, 1)
    return low * LARGEST_SHIFT - skipped + high


def message_table(count):
    table = []
    for shifts in shift_choices():
        bits = message_bits(count, shifts)
        for pairs in rounds_of(count, shifts):
            row = [0] * count
            for edge in pairs:
                row[edge[1]] = bits[edge]
            table.append(row)
    return np.asarray(table, np.int32).reshape(-1)


def finish_kernel(packed, lesser_ref):
    save(lesser_ref, unpack(packed[...]))


def exchange(packed, spare, which):
    count, size = lax.axis_size("energy"), packed.shape[-1]

    def branch_of(shifts):
        rounds = rounds_of(count, shifts)

        def branch(block, *spare):
            out = []
            for pairs in rounds:
                out.append(hop(block, "energy", pairs) if pairs else spare[len(out) - 1])
            (lesser,) = call(
                finish_kernel, "finish", [jax.ShapeDtypeStruct((2, size, size), F32)], 64 * size**3,
                {}, [], None, block,
            )
            return (*out, lesser)

        return branch

    return lax.switch(which, [branch_of(shifts) for shifts in shift_choices()], packed, *spare)


def scatter_kernel(table, phonon_fill, phonon_shift, strength, *refs):
    came, refs = refs[:ROUNDS], refs[ROUNDS:]
    out_ref, held, sums_ref, own_out, small, fills, shifts, arrived, settled = refs

    def block_copy(c):
        return pltpu.make_async_copy(came[c], held.at[c], arrived.at[c])

    numbers = [
        pltpu.make_async_copy(source, target, settled.at[index])
        for index, (source, target) in enumerate(
            ((phonon_shift, shifts), (table, small), (phonon_fill, fills))
        )
    ]
    for c in range(2):
        block_copy(c).start()
    for number in numbers:
        number.start()
    for number in numbers:
        number.wait()
    count = lax.axis_size("energy")
    which = choice_of(shifts[0], shifts[1])
    swapped = (shifts[0] > shifts[1]).astype(jnp.int32)
    bits = [small[(which * ROUNDS + c) * count + lax.axis_index("energy")] for c in range(ROUNDS)]

    for c in range(2, ROUNDS):

        @pl.when(bits[c] > 0)
        def _(c=c):
            block_copy(c).start()

    sums_ref[...] = jnp.zeros_like(sums_ref)
    for c in range(ROUNDS):
        if c < 2:
            block_copy(c).wait()

        @pl.when(bits[c] > 0)
        def _(c=c):
            if c >= 2:
                block_copy(c).wait()
            block = held[c]
            for mode in range(2):
                filled = fills[jnp.where(swapped == 1, 1 - mode, mode)]
                up = (bits[c] // 4**mode % 2).astype(F32)
                down = (bits[c] // (2 * 4**mode) % 2).astype(F32)
                sums_ref[mode] += (up * (filled + 1.0) + down * filled) * block

    near, away = strength[swapped], strength[1 - swapped]
    low, high = unpack(sums_ref[0]), unpack(sums_ref[1])
    done = [pltpu.make_async_copy(own_out.at[p], out_ref.at[p], arrived.at[p]) for p in range(2)]
    for part in range(2):
        own_out[part] = near * low[part] + away * high[part]
        done[part].start()
    for part in range(2):
        done[part].wait()


def call(body, name, outs, flops, spaces, scratch, active, *args, far_outs=(), small_outs=(), aliases=None):
    fetched = [index for index in range(len(args)) if spaces.get(index) is FETCH]
    where = [
        pl.BlockSpec(memory_space=FAR if index in fetched else spaces.get(index, pltpu.VMEM))
        for index in range(len(args))
    ]
    buffers = [pltpu.VMEM(args[index].shape, args[index].dtype) for index in fetched]
    arrivals = [pltpu.SemaphoreType.DMA((len(fetched),))] if fetched else []

    def whole(*refs):
        given, rest = list(refs[: len(args)]), refs[len(args) :]
        own = rest[len(outs) + len(scratch) :]
        rest = rest[: len(outs) + len(scratch)]

        def copies():
            return [
                pltpu.make_async_copy(refs[index], own[slot], own[-1].at[slot])
                for slot, index in enumerate(fetched)
            ]

        def run():
            for copy in copies():
                copy.start()
            for copy in copies():
                copy.wait()
            for slot, index in enumerate(fetched):
                given[index] = own[slot]
            body(*given, *rest)

        if active is None:
            run()
        else:
            pl.when(active())(run)

    made = pl.pallas_call(
        whole,
        out_shape=outs,
        in_specs=where,
        out_specs=[
            pl.BlockSpec(
                memory_space=FAR if index in far_outs else pltpu.SMEM if index in small_outs else pltpu.VMEM
            )
            for index in range(len(outs))
        ],
        scratch_shapes=list(scratch) + buffers + arrivals,
        input_output_aliases=aliases or {},
        compiler_params=pltpu.CompilerParams(vmem_limit_bytes=24 << 20),
        cost_estimate=pl.CostEstimate(flops=flops, bytes_accessed=4 << 20, transcendentals=0),
        name=name,
    )(*[
        pltpu.with_memory_space_constraint(arg, FAR)
        if where[index].memory_space in (FAR, pltpu.SMEM)
        else arg
        for index, arg in enumerate(args)
    ])
    return made


def hop(block, axis, pairs):
    return lax.ppermute(block, axis, pairs)


def on_device(
    hamilton, couple, lead_left, rates, fill, sigma_less, strength, phonon_fill, phonon_shift
):
    e_dev, s_dev, _, size, _ = sigma_less.shape
    n_slab = lax.axis_size("slab")
    assert e_dev == 1 and s_dev == 1 and n_slab == 4
    step_width = ESPAN / (e_dev * lax.axis_size("energy"))
    full = jax.ShapeDtypeStruct((2, size, size), F32)
    half = jax.ShapeDtypeStruct((size, size), F32)
    block = pltpu.VMEM((2, size, size), F32)
    inward = [(0, 1), (3, 2)]
    across_middle = [(1, 2), (2, 1)]
    outward = [(1, 0), (2, 3)]
    unit = 24 * size**3

    def first_body(*refs):
        first_kernel(step_width, *refs)

    def ready_body(*refs):
        ready_kernel(step_width, *refs)

    triple = jax.ShapeDtypeStruct((3, size, size), F32)
    (which,) = call(
        choose_kernel, "choose", [jax.ShapeDtypeStruct((1,), jnp.int32)], 8, {0: pltpu.SMEM}, [],
        None, phonon_shift, small_outs=(0,),
    )
    sent, green, outer_source = call(
        first_body, "first", [triple, full, half], 11 * unit,
        {**dict.fromkeys(range(5), FAR), 5: pltpu.SMEM},
        [block, block, block, pltpu.VMEM((1, size), F32), block, block, pltpu.SemaphoreType.DMA((6,))],
        is_outer, hamilton, couple, lead_left, rates, sigma_less, fill.T,
    )
    came = hop(sent, "slab", inward)
    bare, couple_near = call(
        ready_body, "ready", [full] * 2, unit, dict.fromkeys(range(3), FETCH), [],
        is_inner, hamilton, rates, couple,
    )
    less, across, right = call(
        outer_less_kernel, "outer_less", [full] * 3, 4 * unit, {0: FETCH}, [],
        is_outer, couple, green, outer_source,
    )
    came, which = lax.optimization_barrier((came, which))
    matrix, inner_green, sent = call(
        second_kernel, "second", [full] * 3, 10 * unit, {}, [], is_inner, bare, couple_near, came
    )
    edge = hop(sent, "slab", across_middle)
    source, sent = call(
        second_less_kernel, "second_less", [full, half], 6 * unit, {0: FETCH}, [],
        is_inner, sigma_less, couple_near, came, inner_green,
    )
    edge_less = hop(sent, "slab", across_middle)
    edge, sent = lax.optimization_barrier((edge, sent))
    inner_green, sent = call(
        third_kernel, "third", [full] * 2, 8 * unit, {}, [block], is_inner, matrix, edge, couple_near
    )
    came_green = hop(sent, "slab", outward)
    own_packed, sent = call(
        third_less_kernel, "third_less", [half] * 2, 4 * unit, {}, [block],
        is_inner, source, edge_less, couple_near, inner_green,
    )
    came_less = hop(sent, "slab", outward)
    (base,) = call(
        mixed_kernel, "mixed", [full], 2 * unit, {}, [],
        is_outer, across, right, less, came_green,
    )
    packed, *spare = call(
        last_kernel, "last", [half] * ROUNDS, 2 * unit, {}, [],
        is_outer, across, base, came_less, own_packed, far_outs=range(1, ROUNDS), aliases={3: 0},
    )
    table = message_table(lax.axis_size("energy"))
    *around, lesser = exchange(packed, spare, which[0])
    (scatter,) = call(
        scatter_kernel, "scatter", [full], unit // 8,
        {0: FAR, 1: FAR, 2: FAR, **dict.fromkeys(range(4, 4 + ROUNDS), FAR)},
        [
            pltpu.VMEM((ROUNDS, size, size), F32), block, block,
            pltpu.SMEM(table.shape, jnp.int32), pltpu.SMEM((2,), F32), pltpu.SMEM((2,), jnp.int32),
            pltpu.SemaphoreType.DMA((ROUNDS,)), pltpu.SemaphoreType.DMA((3,)),
        ],
        None, table, phonon_fill, phonon_shift, strength,
        *around, far_outs=(0,),
    )
    return (lesser[None, None], scatter[None, None])


def solution(mesh):
    return jax.shard_map(
        on_device,
        mesh=mesh,
        in_specs=(
            P("slab", None, None, None),
            P("slab", None, None, None),
            P(),
            P("energy", "slab", None),
            P(None, "energy"),
            P("energy", "slab", None, None, None),
            P(),
            P(),
            P(),
        ),
        out_specs=(P("energy", "slab", None, None, None), P("energy", "slab", None, None, None)),
        check_vma=False,
    )
```

```python
import jax
import jax.numpy as jnp
import numpy as np
from jax import lax
from jax.experimental import pallas as pl
from jax.experimental.pallas import tpu as pltpu
from jax.sharding import PartitionSpec as P

ETA = 0.2
EMIN = -2.5
ESPAN = 5.0
LARGEST_SHIFT = 6
POLY_STEPS = 4
POLY_RANGE = 45.0
NORM_SHARE = 5.0
ACCEPT = 2e-3
SLOW_STEPS = 80
ROUNDS = 4
FETCH = "fetch"
FAR = pltpu.MemorySpace.HBM

F32 = jnp.float32
BF16 = jnp.bfloat16


def dot(a, b):
    return jnp.dot(a, b, preferred_element_type=F32)


def dot_nt(a, b):
    return lax.dot_general(a, b, (((1,), (1,)), ((), ())), preferred_element_type=F32)


def dot_tn(a, b):
    return lax.dot_general(a, b, (((0,), (0,)), ((), ())), preferred_element_type=F32)


def cols(*parts):
    return jnp.concatenate(parts, axis=1)


def rows(*parts):
    return jnp.concatenate(parts, axis=0)


def split(pair):
    high = tuple(part.astype(BF16) for part in pair)
    low = tuple((part - top.astype(F32)).astype(BF16) for part, top in zip(pair, high))
    return high, low


def rounded(pair):
    return tuple(part.astype(BF16) for part in pair)


def left_form(pair):
    return cols(pair[0], pair[1])


def right_form(pair):
    return rows(cols(pair[0], pair[1]), cols(-pair[1], pair[0]))


def halves_cols(wide):
    size = wide.shape[1] // 2
    return wide[:, :size], wide[:, size:]


def halves_rows(tall):
    size = tall.shape[0] // 2
    return tall[:size], tall[size:]


def product_one(a, b):
    return halves_cols(dot(left_form(a), right_form(b)))


def product_split(a_high, a_low, b_high, b_low):
    top, right = left_form(a_high), right_form(b_high)
    return halves_cols(
        dot(cols(top, top, left_form(a_low)), rows(right, right_form(b_low), right))
    )


def product(a, b):
    return product_split(*split(a), *split(b))


def product_two(a, b, c):
    a_high, a_low = split(a)
    top, low = left_form(a_high), left_form(a_low)

    def tall(pair):
        high, rest = split(pair)
        right = right_form(high)
        return rows(right, right_form(rest), right)

    both = dot(cols(top, top, low), cols(tall(b), tall(c)))
    size = both.shape[1] // 2
    return halves_cols(both[:, :size]), halves_cols(both[:, size:])


def product_nt(a, b):
    def stacked(pair):
        return rows(cols(pair[0], pair[1]), cols(pair[1], -pair[0]))

    a_high, a_low = split(a)
    b_high, b_low = split(b)
    top, right = stacked(a_high), left_form(b_high)
    return halves_rows(
        dot_nt(cols(top, top, stacked(a_low)), cols(right, left_form(b_low), right))
    )


def product_tn(a, b):
    def tall(pair):
        return rows(pair[0], pair[1])

    def stacked(pair):
        return rows(cols(pair[0], pair[1]), cols(pair[1], -pair[0]))

    a_high, a_low = split(a)
    b_high, b_low = split(b)
    top, right = tall(a_high), stacked(b_high)
    return halves_cols(
        dot_tn(rows(top, top, tall(a_low)), rows(right, stacked(b_low), right))
    )


def minus(a, b):
    return (a[0] - b[0], a[1] - b[1])


def plus(a, b):
    return (a[0] + b[0], a[1] + b[1])


def dagger(a):
    return (a[0].T, -a[1].T)


def load(ref):
    return (ref[0], ref[1])


def save(ref, pair):
    ref[0] = pair[0]
    ref[1] = pair[1]


def square_sum(pair):
    return jnp.sum(pair[0] * pair[0] + pair[1] * pair[1])


def row_col(size):
    shape = (size, size)
    return lax.broadcasted_iota(jnp.int32, shape, 0), lax.broadcasted_iota(jnp.int32, shape, 1)


def identity(size):
    row, col = row_col(size)
    return (row == col).astype(F32)


def pack(pair):
    row, col = row_col(pair[0].shape[0])
    return jnp.where(row > col, pair[0], pair[1])


def unpack(packed):
    row, col = row_col(packed.shape[0])
    flipped = packed.T
    real = jnp.where(row > col, packed, jnp.where(row < col, -flipped, 0.0))
    imag = jnp.where(row > col, flipped, packed)
    return (real, imag)


def scalings():
    low, high, found = 1.0 / POLY_RANGE, 1.0, []
    for _ in range(POLY_STEPS):
        rate = (high - low) / (high + low)
        found.append(2.0 / (low + high))
        low, high = 1.0 - rate * rate, 1.0
    return found


def invert(matrix, out_ref):
    size = matrix[0].shape[0]
    high, low = split(matrix)
    adjoint = dagger(matrix)
    adjoint_16 = rounded(adjoint)
    state = product_one(adjoint_16, high)
    state_16 = rounded(state)
    inverse_bound = NORM_SHARE * lax.rsqrt(square_sum(state))
    both = dot(left_form(state_16), cols(right_form(state_16), right_form(adjoint_16)))
    squared = halves_cols(both[:, : 2 * size])
    moved = halves_cols(both[:, 2 * size :])
    scales = scalings()
    once, twice = 2.0 * scales[0] * inverse_bound, scales[0] ** 2 * inverse_bound**2
    guess = tuple(once * a - twice * q for a, q in zip(adjoint, moved))
    state = tuple(once * s - twice * q for s, q in zip(state, squared))
    for step in range(1, POLY_STEPS):
        once, twice = 2.0 * scales[step], scales[step] ** 2
        state_16, guess_16 = rounded(state), rounded(guess)
        if step < POLY_STEPS - 1:
            both = dot(left_form(state_16), cols(right_form(state_16), right_form(guess_16)))
            squared = halves_cols(both[:, : 2 * size])
            moved = halves_cols(both[:, 2 * size :])
            state = tuple(once * s - twice * q for s, q in zip(state, squared))
        else:
            moved = product_one(state_16, guess_16)
        guess = tuple(once * g - twice * q for g, q in zip(guess, moved))
    guess_high, guess_low = split(guess)
    made = product_split(high, low, guess_high, guess_low)
    residual = (identity(size) - made[0], -made[1])
    residual_16 = rounded(residual)
    second = product_one(residual_16, residual_16)
    better = plus(guess, product_one(guess_high, residual_16))
    save(out_ref, plus(better, product_one(rounded(better), rounded(second))))
    good = square_sum(second) < ACCEPT

    @pl.when(jnp.logical_not(good))
    def _():
        square = product(adjoint, matrix)
        bound = jnp.sqrt(square_sum(square))
        save(out_ref, (adjoint[0] / bound, adjoint[1] / bound))

        def more(carry):
            step, left_over = carry
            return jnp.logical_and(step < SLOW_STEPS, jnp.logical_not(left_over < 1e-6))

        def refine(carry):
            step, _ = carry
            now = load(out_ref)
            made = product(matrix, now)
            residual = (identity(size) - made[0], -made[1])
            save(out_ref, plus(now, product(now, residual)))
            return step + 1, square_sum(residual)

        lax.while_loop(more, refine, (jnp.int32(0), jnp.float32(1e30)))


def is_outer():
    place = lax.axis_index("slab")
    return jnp.logical_or(place == 0, place == lax.axis_size("slab") - 1)


def is_inner():
    return jnp.logical_not(is_outer())


def on_left():
    return lax.axis_index("slab") < lax.axis_size("slab") // 2


def bare_matrix(step_width, hamilton, rates):
    size = hamilton[0].shape[-1]
    energy = lax.axis_index("energy").astype(F32) * step_width + EMIN
    eye = identity(size)
    return (energy * eye - hamilton[0], (ETA + rates[...]) * eye - hamilton[1])


def choose_kernel(phonon_shift, which):
    which[0] = choice_of(phonon_shift[0], phonon_shift[1])


def first_kernel(
    step_width, hamilton, couple, lead_left, rates, sigma, fill, send_ref, green_ref, source_ref,
    own_ham, own_lead, own_couple, own_rates, own_sigma, own_green, arrived,
):
    first = lax.axis_index("slab") == 0

    def fetch(source, target, index):
        return pltpu.make_async_copy(source, target, arrived.at[index])

    @pl.when(first)
    def _():
        fetch(lead_left, own_lead, 0).start()

    @pl.when(jnp.logical_not(first))
    def _():
        fetch(couple.at[0], own_lead, 0).start()

    fetch(rates.at[0], own_rates, 2).start()
    fetch(hamilton.at[0], own_ham, 1).start()
    fetch(lead_left, own_lead, 0).wait()
    fetch(sigma.at[0, 0], own_sigma, 3).start()

    @pl.when(first)
    def _():
        fetch(couple.at[0], own_couple, 4).start()

    lead = load(own_lead)
    gamma = product_nt(lead, lead)
    fetch(hamilton.at[0], own_ham, 1).wait()
    fetch(rates.at[0], own_rates, 2).wait()
    real, imag = bare_matrix(step_width, load(own_ham), own_rates)
    save(own_lead, gamma)
    invert((real - 0.5 * gamma[1], imag + 0.5 * gamma[0]), own_green)
    save(green_ref, load(own_green))
    fetch(sigma.at[0, 0], own_sigma, 3).wait()
    occupation = jnp.where(first, fill[0, 0], fill[0, 1])
    save(
        own_sigma, (own_sigma[0] - occupation * own_lead[1], own_sigma[1] + occupation * own_lead[0])
    )
    source_ref[...] = pack(load(own_sigma))

    @pl.when(first)
    def _():
        fetch(couple.at[0], own_couple, 4).wait()
        own = load(own_couple)
        right = product_tn(own, load(own_green))
        edge, moved = product_two(right, own, load(own_sigma))
        save(send_ref, edge)
        send_ref[2] = pack(product_nt(moved, right))

    @pl.when(jnp.logical_not(first))
    def _():
        save(send_ref, load(own_green))
        send_ref[2] = source_ref[...]


def outer_less_kernel(couple, green_ref, source_ref, less_ref, across_ref, right_ref):
    green = load(green_ref)
    less = product_nt(product(green, unpack(source_ref[...])), green)
    save(less_ref, less)

    @pl.when(on_left())
    def _():
        own = load(couple.at[0])
        save(across_ref, product(green, own))
        save(right_ref, product_tn(own, less))

    @pl.when(jnp.logical_not(on_left()))
    def _():
        save(across_ref, green)
        save(right_ref, less)


def ready_kernel(step_width, hamilton, rates, couple, matrix_ref, couple_ref):
    save(matrix_ref, bare_matrix(step_width, load(hamilton.at[0]), rates.at[0]))
    save(couple_ref, load(couple.at[0]))


def second_kernel(matrix_in, couple, came, matrix_ref, green_ref, send_ref):
    edge = (came[0], came[1])

    @pl.when(on_left())
    def _():
        save(matrix_ref, minus(load(matrix_in), edge))

    @pl.when(jnp.logical_not(on_left()))
    def _():
        own = load(couple)
        save(matrix_ref, minus(load(matrix_in), product_nt(product(own, edge), own)))

    invert(load(matrix_ref), green_ref)

    @pl.when(on_left())
    def _():
        own = load(couple)
        save(send_ref, product(product_tn(own, load(green_ref)), own))

    @pl.when(jnp.logical_not(on_left()))
    def _():
        save(send_ref, load(green_ref))


def second_less_kernel(sigma, couple, came, green_ref, source_ref, send_ref):
    outside = unpack(came[2])
    own_sigma = (sigma[0, 0, 0], sigma[0, 0, 1])

    @pl.when(on_left())
    def _():
        save(source_ref, plus(own_sigma, outside))

    @pl.when(jnp.logical_not(on_left()))
    def _():
        inside = product(load(couple), (came[0], came[1]))
        save(source_ref, plus(own_sigma, product_nt(product(inside, outside), inside)))

    green = load(green_ref)
    less = product_nt(product(green, load(source_ref)), green)

    @pl.when(on_left())
    def _():
        own = load(couple)
        send_ref[...] = pack(product(product_tn(own, less), own))

    @pl.when(jnp.logical_not(on_left()))
    def _():
        send_ref[...] = pack(less)


def third_kernel(matrix_in, edge, couple, green_ref, send_ref, matrix_ref):
    @pl.when(on_left())
    def _():
        own = load(couple)
        around = product_nt(product(own, load(edge)), own)
        save(matrix_ref, minus(load(matrix_in), around))

    @pl.when(jnp.logical_not(on_left()))
    def _():
        save(matrix_ref, minus(load(matrix_in), load(edge)))

    invert(load(matrix_ref), green_ref)

    @pl.when(on_left())
    def _():
        save(send_ref, load(green_ref))

    @pl.when(jnp.logical_not(on_left()))
    def _():
        own = load(couple)
        save(send_ref, product(product_tn(own, load(green_ref)), own))


def third_less_kernel(source, edge, couple, green_ref, own_ref, send_ref, total_ref):
    came = unpack(edge[...])

    @pl.when(on_left())
    def _():
        own = load(couple)
        save(total_ref, plus(load(source), product_nt(product(own, came), own)))

    @pl.when(jnp.logical_not(on_left()))
    def _():
        save(total_ref, plus(load(source), came))

    green = load(green_ref)
    less = product_nt(product(green, load(total_ref)), green)
    own_ref[...] = pack(less)

    @pl.when(on_left())
    def _():
        send_ref[...] = pack(less)

    @pl.when(jnp.logical_not(on_left()))
    def _():
        own = load(couple)
        send_ref[...] = pack(product(product_tn(own, less), own))


def mixed_kernel(across_ref, right_ref, less_ref, inner_green, base_ref):
    mixed = product(product(load(across_ref), load(inner_green)), load(right_ref))
    save(base_ref, minus(plus(load(less_ref), mixed), dagger(mixed)))


def last_kernel(across_ref, base_ref, inner_less, own_packed, packed_ref, *_):
    across = load(across_ref)
    packed_ref[...] = pack(
        plus(load(base_ref), product_nt(product(across, unpack(inner_less[...])), across))
    )


def message_bits(count, shifts):
    found = {}
    for mode, shift in enumerate(shifts):
        for place in range(count - shift):
            for edge, bit in (((place + shift, place), 0), ((place, place + shift), 1)):
                found[edge] = found.get(edge, 0) | 1 << (2 * mode + bit)
    return found


def rounds_of(count, shifts):
    moves = []
    for shift in sorted(set(shifts)):
        moves.append([(place + shift, place) for place in range(count - shift)])
        moves.append([(place, place + shift) for place in range(count - shift)])

    def fits(pairs, more):
        return all({p[end] for p in pairs}.isdisjoint({p[end] for p in more}) for end in range(2))

    def placed(index, rounds):
        if index == len(moves):
            return rounds
        found = [
            placed(index + 1, rounds[:r] + [rounds[r] + moves[index]] + rounds[r + 1 :])
            for r in range(len(rounds))
            if fits(rounds[r], moves[index])
        ]
        found.append(placed(index + 1, rounds + [moves[index]]))
        return min(found, key=len)

    best = placed(0, [])
    return best + [[]] * (ROUNDS - len(best))


def shift_choices():
    return [(a, b) for a in range(1, LARGEST_SHIFT + 1) for b in range(a, LARGEST_SHIFT + 1)]


def choice_of(first, second):
    low = jnp.minimum(first, second) - 1
    high = jnp.maximum(first, second) - 1
    skipped = low * (low + 1)
    skipped = jnp.right_shift(skipped, 1)
    return low * LARGEST_SHIFT - skipped + high


def message_table(count):
    table = []
    for shifts in shift_choices():
        bits = message_bits(count, shifts)
        for pairs in rounds_of(count, shifts):
            row = [0] * count
            for edge in pairs:
                row[edge[1]] = bits[edge]
            table.append(row)
    return np.asarray(table, np.int32).reshape(-1)


def finish_kernel(packed, lesser_ref):
    save(lesser_ref, unpack(packed[...]))


def exchange(packed, spare, which):
    count, size = lax.axis_size("energy"), packed.shape[-1]

    def branch_of(shifts):
        rounds = rounds_of(count, shifts)

        def branch(block, *spare):
            out = []
            for pairs in rounds:
                out.append(hop(block, "energy", pairs) if pairs else spare[len(out) - 1])
            (lesser,) = call(
                finish_kernel, "finish", [jax.ShapeDtypeStruct((2, size, size), F32)], 64 * size**3,
                {}, [], None, block,
            )
            return (*out, lesser)

        return branch

    return lax.switch(which, [branch_of(shifts) for shifts in shift_choices()], packed, *spare)


def scatter_kernel(table, phonon_fill, phonon_shift, strength, *refs):
    came, refs = refs[:ROUNDS], refs[ROUNDS:]
    out_ref, held, sums_ref, own_out, small, fills, shifts, arrived, settled = refs

    def block_copy(c):
        return pltpu.make_async_copy(came[c], held.at[c], arrived.at[c])

    numbers = [
        pltpu.make_async_copy(source, target, settled.at[index])
        for index, (source, target) in enumerate(
            ((phonon_shift, shifts), (table, small), (phonon_fill, fills))
        )
    ]
    for c in range(2):
        block_copy(c).start()
    for number in numbers:
        number.start()
    for number in numbers:
        number.wait()
    count = lax.axis_size("energy")
    which = choice_of(shifts[0], shifts[1])
    swapped = (shifts[0] > shifts[1]).astype(jnp.int32)
    bits = [small[(which * ROUNDS + c) * count + lax.axis_index("energy")] for c in range(ROUNDS)]

    for c in range(2, ROUNDS):

        @pl.when(bits[c] > 0)
        def _(c=c):
            block_copy(c).start()

    sums_ref[...] = jnp.zeros_like(sums_ref)
    for c in range(ROUNDS):
        if c < 2:
            block_copy(c).wait()

        @pl.when(bits[c] > 0)
        def _(c=c):
            if c >= 2:
                block_copy(c).wait()
            block = held[c]
            for mode in range(2):
                filled = fills[jnp.where(swapped == 1, 1 - mode, mode)]
                up = (bits[c] // 4**mode % 2).astype(F32)
                down = (bits[c] // (2 * 4**mode) % 2).astype(F32)
                sums_ref[mode] += (up * (filled + 1.0) + down * filled) * block

    near, away = strength[swapped], strength[1 - swapped]
    low, high = unpack(sums_ref[0]), unpack(sums_ref[1])
    done = [pltpu.make_async_copy(own_out.at[p], out_ref.at[p], arrived.at[p]) for p in range(2)]
    for part in range(2):
        own_out[part] = near * low[part] + away * high[part]
        done[part].start()
    for part in range(2):
        done[part].wait()


def call(body, name, outs, flops, spaces, scratch, active, *args, far_outs=(), small_outs=(), aliases=None):
    fetched = [index for index in range(len(args)) if spaces.get(index) is FETCH]
    where = [
        pl.BlockSpec(memory_space=FAR if index in fetched else spaces.get(index, pltpu.VMEM))
        for index in range(len(args))
    ]
    buffers = [pltpu.VMEM(args[index].shape, args[index].dtype) for index in fetched]
    arrivals = [pltpu.SemaphoreType.DMA((len(fetched),))] if fetched else []

    def whole(*refs):
        given, rest = list(refs[: len(args)]), refs[len(args) :]
        own = rest[len(outs) + len(scratch) :]
        rest = rest[: len(outs) + len(scratch)]

        def copies():
            return [
                pltpu.make_async_copy(refs[index], own[slot], own[-1].at[slot])
                for slot, index in enumerate(fetched)
            ]

        def run():
            for copy in copies():
                copy.start()
            for copy in copies():
                copy.wait()
            for slot, index in enumerate(fetched):
                given[index] = own[slot]
            body(*given, *rest)

        if active is None:
            run()
        else:
            pl.when(active())(run)

    made = pl.pallas_call(
        whole,
        out_shape=outs,
        in_specs=where,
        out_specs=[
            pl.BlockSpec(
                memory_space=FAR if index in far_outs else pltpu.SMEM if index in small_outs else pltpu.VMEM
            )
            for index in range(len(outs))
        ],
        scratch_shapes=list(scratch) + buffers + arrivals,
        input_output_aliases=aliases or {},
        compiler_params=pltpu.CompilerParams(vmem_limit_bytes=24 << 20),
        cost_estimate=pl.CostEstimate(flops=flops, bytes_accessed=4 << 20, transcendentals=0),
        name=name,
    )(*[
        pltpu.with_memory_space_constraint(arg, FAR)
        if where[index].memory_space in (FAR, pltpu.SMEM)
        else arg
        for index, arg in enumerate(args)
    ])
    return made


def hop(block, axis, pairs):
    return lax.ppermute(block, axis, pairs)


def on_device(
    hamilton, couple, lead_left, rates, fill, sigma_less, strength, phonon_fill, phonon_shift
):
    e_dev, s_dev, _, size, _ = sigma_less.shape
    n_slab = lax.axis_size("slab")
    assert e_dev == 1 and s_dev == 1 and n_slab == 4
    step_width = ESPAN / (e_dev * lax.axis_size("energy"))
    full = jax.ShapeDtypeStruct((2, size, size), F32)
    half = jax.ShapeDtypeStruct((size, size), F32)
    block = pltpu.VMEM((2, size, size), F32)
    inward = [(0, 1), (3, 2)]
    across_middle = [(1, 2), (2, 1)]
    outward = [(1, 0), (2, 3)]
    unit = 24 * size**3

    def first_body(*refs):
        first_kernel(step_width, *refs)

    def ready_body(*refs):
        ready_kernel(step_width, *refs)

    triple = jax.ShapeDtypeStruct((3, size, size), F32)
    (which,) = call(
        choose_kernel, "choose", [jax.ShapeDtypeStruct((1,), jnp.int32)], 8, {0: pltpu.SMEM}, [],
        None, phonon_shift, small_outs=(0,),
    )
    sent, green, outer_source = call(
        first_body, "first", [triple, full, half], 11 * unit,
        {**dict.fromkeys(range(5), FAR), 5: pltpu.SMEM},
        [block, block, block, pltpu.VMEM((1, size), F32), block, block, pltpu.SemaphoreType.DMA((6,))],
        is_outer, hamilton, couple, lead_left, rates, sigma_less, fill.T,
    )
    came = hop(sent, "slab", inward)
    bare, couple_near = call(
        ready_body, "ready", [full] * 2, unit, dict.fromkeys(range(3), FETCH), [],
        is_inner, hamilton, rates, couple,
    )
    less, across, right = call(
        outer_less_kernel, "outer_less", [full] * 3, 4 * unit, {0: FETCH}, [],
        is_outer, couple, green, outer_source,
    )
    came, which = lax.optimization_barrier((came, which))
    matrix, inner_green, sent = call(
        second_kernel, "second", [full] * 3, 10 * unit, {}, [], is_inner, bare, couple_near, came
    )
    edge = hop(sent, "slab", across_middle)
    source, sent = call(
        second_less_kernel, "second_less", [full, half], 6 * unit, {0: FETCH}, [],
        is_inner, sigma_less, couple_near, came, inner_green,
    )
    edge_less = hop(sent, "slab", across_middle)
    edge, sent = lax.optimization_barrier((edge, sent))
    inner_green, sent = call(
        third_kernel, "third", [full] * 2, 8 * unit, {}, [block], is_inner, matrix, edge, couple_near
    )
    came_green = hop(sent, "slab", outward)
    own_packed, sent = call(
        third_less_kernel, "third_less", [half] * 2, 4 * unit, {}, [block],
        is_inner, source, edge_less, couple_near, inner_green,
    )
    came_less = hop(sent, "slab", outward)
    (base,) = call(
        mixed_kernel, "mixed", [full], 2 * unit, {}, [],
        is_outer, across, right, less, came_green,
    )
    packed, *spare = call(
        last_kernel, "last", [half] * ROUNDS, 2 * unit, {}, [],
        is_outer, across, base, came_less, own_packed, far_outs=range(1, ROUNDS), aliases={3: 0},
    )
    table = message_table(lax.axis_size("energy"))
    *around, lesser = exchange(packed, spare, which[0])
    (scatter,) = call(
        scatter_kernel, "scatter", [full], unit // 8,
        {0: FAR, 1: FAR, 2: FAR, **dict.fromkeys(range(4, 4 + ROUNDS), FAR)},
        [
            pltpu.VMEM((ROUNDS, size, size), F32), block, block,
            pltpu.SMEM(table.shape, jnp.int32), pltpu.SMEM((2,), F32), pltpu.SMEM((2,), jnp.int32),
            pltpu.SemaphoreType.DMA((ROUNDS,)), pltpu.SemaphoreType.DMA((3,)),
        ],
        None, table, phonon_fill, phonon_shift, strength,
        *around, far_outs=(0,),
    )
    return (lesser[None, None], scatter[None, None])


def solution(mesh):
    return jax.shard_map(
        on_device,
        mesh=mesh,
        in_specs=(
            P("slab", None, None, None),
            P("slab", None, None, None),
            P(),
            P("energy", "slab", None),
            P(None, "energy"),
            P("energy", "slab", None, None, None),
            P(),
            P(),
            P(),
        ),
        out_specs=(P("energy", "slab", None, None, None), P("energy", "slab", None, None, None)),
        check_vma=False,
    )
```
